32 devices in a mesh: stream: 2 (over y), docs: 16 (over z, x, core).
Axes of the slice: x: 2, y: 2, z: 4, core: 2. Of those that a mesh axis runs over, the one named last changes fastest.
Arguments:
- block_features: bfloat16 [2, 8192, 768], P('stream', 'docs'), may hold values from -6 to 6
- cotangent: bfloat16 [2, 8192, 768], P('stream', 'docs'), may hold values from -6 to 6
- text_counts: int32 [16, 2], P('docs'), may hold values from 64 to 448, as said below
- visual_counts: int32 [16, 2], P('docs'), may hold values from 1 to 89, as said below
- w_cross_q: bfloat16 [2, 768, 768], P('stream'), may hold values from -0.21875 to 0.21875
- w_cross_kv: bfloat16 [2, 768, 1536], P('stream'), may hold values from -0.21875 to 0.21875
- w_cross_out: bfloat16 [2, 768, 768], P('stream'), may hold values from -1.25 to 1.25
- w_self_qkv: bfloat16 [2, 768, 2304], P('stream'), may hold values from -0.21875 to 0.21875
- w_self_out: bfloat16 [2, 768, 768], P('stream'), may hold values from -1.75 to 1.75
- w_ffn_in: bfloat16 [2, 768, 3072], P('stream'), may hold values from -0.21875 to 0.21875
- w_ffn_out: bfloat16 [2, 3072, 768], P('stream'), may hold values from -0.109375 to 0.109375
- w_gate: bfloat16 [2, 1536, 768], P('stream'), may hold values from -0.15625 to 0.15625
- ln_gain: bfloat16 [2, 3, 768], P('stream'), may hold values from 0.5 to 1.5
- ln_bias: bfloat16 [2, 3, 768], P('stream'), may hold values from -3 to 3
- gate_bias: bfloat16 [2, 768], P('stream'), may hold values from -3 to 3
Outputs:
- combined: float32 [2, 8192, 768], P('stream', 'docs')
- input_grad: float32 [2, 8192, 768], P('stream', 'docs')
- grad_cross_q: float32 [2, 768, 768], P('stream', 'docs')
- grad_cross_kv: float32 [2, 768, 1536], P('stream', 'docs')
- grad_cross_out: float32 [2, 768, 768], P('stream', 'docs')
- grad_self_qkv: float32 [2, 768, 2304], P('stream', 'docs')
- grad_self_out: float32 [2, 768, 768], P('stream', 'docs')
- grad_ffn_in: float32 [2, 768, 3072], P('stream', 'docs')
- grad_ffn_out: float32 [2, 3072, 768], P('stream', 'docs')
- grad_gate: float32 [2, 1536, 768], P('stream', 'docs')
- grad_ln_gain: float32 [2, 3, 768], P('stream', None, 'docs')
- grad_ln_bias: float32 [2, 3, 768], P('stream', None, 'docs')
- grad_gate_bias: float32 [2, 768], P('stream', 'docs')
The draws below stay inside these ranges and needn't reach their ends.
Inputs may be any that keep to these rules, and one draw needn't show every extreme that they name: `text_counts`: the 2 text counts of one group of 512 rows sum to 512. `visual_counts`: each document has at least one visual block and no more visual blocks than text blocks.
All inputs are finite; a program needn't handle non-finite values.
Results may differ from the reference program's by a relative error of at most 0.025.
Values may be sent and summed in bfloat16 or wider, within the bound.
No kernel may reach another device: no remote copies, remote signals or barrier semaphores. Data moves between devices by JAX's collectives and lax.ppermute only.
A program may use at most 192 MiB of HBM per device.

```python
import jax
import jax.numpy as jnp
from jax import lax

D = 768
HD = 64
FF = 3072
TOK_DEV = 512
DOCS_DEV = 2
TOKENS = 8192
N_DOCS = 16


def draw_layout(key):
    weight_key = jax.random.fold_in(key, 11)
    count_key = jax.random.fold_in(key, 12)
    group_key = jax.random.fold_in(key, 13)
    chosen = jax.random.randint(group_key, (), 0, N_DOCS).astype(jnp.int32)
    row_ids = jnp.arange(N_DOCS, dtype=jnp.int32)[:, None]
    col_ids = jnp.arange(DOCS_DEV, dtype=jnp.int32)[None, :]
    is_chosen = row_ids == chosen
    forced = (col_ids == DOCS_DEV - 1).astype(jnp.int32)
    pieces = jax.random.randint(weight_key, (N_DOCS, DOCS_DEV), 1, 9).astype(jnp.int32)
    pieces = jnp.where(is_chosen, forced, pieces).astype(jnp.int32)
    floor_len = TOK_DEV // (4 * DOCS_DEV)
    spare = TOK_DEV - floor_len * DOCS_DEV
    running = jnp.cumsum(pieces, axis=1).astype(jnp.int32)
    whole_sum = running[:, -1:]
    cut_points = spare * running // whole_sum
    before = jnp.concatenate([jnp.zeros((N_DOCS, 1), jnp.int32), cut_points[:, :-1]], axis=1)
    text_len = (floor_len + cut_points - before).astype(jnp.int32)
    upper = jnp.maximum(text_len // 5, 1)
    visual_len = jax.random.randint(count_key, (N_DOCS, DOCS_DEV), 1, upper + 1).astype(jnp.int32)
    visual_len = jnp.where(is_chosen & (col_ids == DOCS_DEV - 1), upper, visual_len)
    visual_len = jnp.where(is_chosen & (col_ids == 0), 1, visual_len).astype(jnp.int32)
    return (text_len, visual_len)


def draw_text_counts(key, part):
    return draw_layout(key)[0]


def draw_visual_counts(key, part):
    return draw_layout(key)[1]


def raised(entries, rng, source, target, blocks, factor):
    def block_of(dim):
        return (jnp.arange(entries.shape[dim]) // (entries.shape[dim] // blocks)).reshape((-1,) + (1,) * (entries.ndim - 1 - dim))

    one_side = jax.random.permutation(rng, blocks)[block_of(target)]
    second = (block_of(target) + blocks // 2) % blocks
    return jnp.where((block_of(source) == one_side) | (block_of(source) == second), factor * entries, entries)


def level_of(own_key, extent, cuts, low, high):
    level, own = 1.0, jax.random.fold_in(own_key, 6)
    for axis_at, blocks in cuts:
        heights = jnp.exp(jax.random.uniform(jax.random.fold_in(own, axis_at), (blocks,), jnp.float32, low / len(cuts), high / len(cuts)))
        level = level * jnp.repeat(heights, extent[axis_at] // blocks).reshape([-1 if axis == axis_at else 1 for axis in range(len(extent))])
    return level


def normal_values(rng, dims, scale, reach, cuts=(), kind=jnp.bfloat16):
    values = jax.random.normal(rng, dims, jnp.float32) * scale
    if len(cuts) > 0:
        values = level_of(rng, dims, cuts, -0.22, 0.18) * values
    return jnp.clip(values, min=-reach, max=reach).astype(kind)


def gaussian_with(own_key, shape, width, limit, cuts, heavy, kind=jnp.bfloat16):
    values = width * jax.random.normal(own_key, shape, jnp.float32)
    if cuts:
        values = values * level_of(own_key, shape, cuts, -0.22, 0.18)
    return jnp.clip(raised(values, jax.random.fold_in(own_key, 3), *heavy), -limit, limit).astype(kind)


def setup_inputs(seed: int = 0) -> dict:
    key_of = jax.random.split(jax.random.key(seed), 16)
    return {
        "block_features": normal_values(key_of[0], (2, TOKENS, D), 1.0, 6.0, ((0, 2), (1, 16))),
        "cotangent": gaussian_with(key_of[1], (2, TOKENS, D), 1.0, 6.0, ((0, 2), (1, 16)), (1, 2, 16, 2.0)),
        "text_counts": draw_text_counts(jax.random.fold_in(key_of[15], 71), 0),
        "visual_counts": draw_visual_counts(jax.random.fold_in(key_of[15], 71), 0),
        "w_cross_q": normal_values(key_of[4], (2, D, D), D ** -0.5, 0.21875, ((0, 2),)),
        "w_cross_kv": normal_values(key_of[5], (2, D, 2 * D), D ** -0.5, 0.21875, ((0, 2),)),
        "w_cross_out": normal_values(key_of[6], (2, D, D), (D // 32) ** -0.5, 1.25, ((0, 2),)),
        "w_self_qkv": normal_values(key_of[7], (2, D, 3 * D), D ** -0.5, 0.21875, ((0, 2),)),
        "w_self_out": normal_values(key_of[8], (2, D, D), (D // 64) ** -0.5, 1.75, ((0, 2),)),
        "w_ffn_in": normal_values(key_of[9], (2, D, FF), D ** -0.5, 0.21875, ((0, 2),)),
        "w_ffn_out": normal_values(key_of[10], (2, FF, D), FF ** -0.5, 0.109375, ((0, 2),)),
        "w_gate": normal_values(key_of[11], (2, 2 * D, D), (2 * D) ** -0.5, 0.15625, ((0, 2),)),
        "ln_gain": jnp.clip(1.0 + 0.1 * jax.random.normal(key_of[12], (2, 3, D), jnp.float32), 0.5, 1.5).astype(jnp.bfloat16),
        "ln_bias": normal_values(key_of[13], (2, 3, D), 0.3, 3.0, ((0, 2),)),
        "gate_bias": normal_values(key_of[14], (2, D), 0.5, 3.0, ((0, 2),)),
    }


@jax.custom_vjp
def low(v):
    return lax.optimization_barrier(v.astype(jnp.bfloat16)).astype(jnp.float32)

@jax.custom_vjp
def low_back(v):
    return v

def low_keep(v):
    return (low(v), None)

def low_pass(kept, grad):
    return (grad,)

def back_keep(v):
    return (v, None)

def back_low(kept, grad):
    return (low(grad),)
low.defvjp(low_keep, low_pass)
low_back.defvjp(back_keep, back_low)
norm_epsilon = 1e-06
masked_value = -1e+30

def matmul(left, right):
    return jnp.dot(left, right, precision=lax.Precision.HIGHEST)

def layer_norm(resid, gain, shift):
    center = resid - lax.optimization_barrier(jnp.mean(resid, axis=-1, keepdims=True))
    spread = lax.optimization_barrier(jnp.mean(center * center, axis=-1, keepdims=True))
    return center * lax.rsqrt(spread + norm_epsilon) * gain + shift

def layout(text_row, visual_row, tokens):
    doc_ends = jnp.cumsum(text_row).astype(jnp.int32)
    doc_starts = (doc_ends - text_row).astype(jnp.int32)
    positions = jnp.arange(tokens, dtype=jnp.int32)
    doc_ids = lax.optimization_barrier(jnp.sum((positions[:, None] >= doc_ends[None, :]).astype(jnp.int32), axis=1)).astype(jnp.int32)
    member = doc_ids[:, None] == jnp.arange(text_row.shape[0], dtype=jnp.int32)[None, :]
    row_start = lax.optimization_barrier(jnp.sum(jnp.where(member, doc_starts[None, :], 0), axis=1)).astype(jnp.int32)
    row_visual = lax.optimization_barrier(jnp.sum(jnp.where(member, visual_row[None, :], 0), axis=1)).astype(jnp.int32)
    visible = positions - row_start < row_visual
    return (doc_ids, visible)

def attention(queries, key_rows, value_rows, allowed):
    tokens = queries.shape[0]
    query_heads = queries.reshape(tokens, -1, HD)
    key_heads = key_rows.reshape(tokens, -1, HD)
    value_heads = value_rows.reshape(tokens, -1, HD)
    raw = jnp.einsum('qhd,khd->hqk', query_heads, key_heads, precision=lax.Precision.HIGHEST) * HD ** (-0.5)
    scores = low_back(jnp.where(allowed[None], raw, masked_value))
    row_max = lax.optimization_barrier(jnp.max(scores, axis=-1, keepdims=True))
    shifted = jnp.exp(scores - row_max)
    attn_probs = shifted / lax.optimization_barrier(jnp.sum(shifted, axis=-1, keepdims=True))
    mixed = jnp.einsum('hqk,khd->qhd', low(attn_probs), value_heads, precision=lax.Precision.HIGHEST)
    return mixed.reshape(tokens, -1)

def group_forward(params, inputs, text_row, visual_row):
    w_cross_q, w_cross_kv, w_cross_out, w_self_qkv, w_self_out, w_ffn_in, w_ffn_out, w_gate, ln_gain, ln_bias, gate_bias = params
    doc_ids, visible = layout(text_row, visual_row, TOK_DEV)
    same_doc = doc_ids[:, None] == doc_ids[None, :]
    valid = (jnp.ones((TOK_DEV,), jnp.float32), visible.astype(jnp.float32))
    sent_kv = [low_back(low(matmul(inputs[half], w_cross_kv[half]))) for half in range(2)]
    thirds = []
    for half in range(2):
        partner = 1 - half
        features = inputs[half]
        queries = low_back(low(matmul(features, w_cross_q[half])))
        cross_keys = sent_kv[partner][:, :D]
        cross_values = sent_kv[partner][:, D:]
        cross_res = attention(queries, cross_keys, cross_values, same_doc & (valid[partner] > 0.5)[None, :])
        branch = low_back(matmul(low_back(low(cross_res)), w_cross_out[half]))
        first_out = layer_norm(features + branch, ln_gain[half, 0], ln_bias[half, 0])
        self_qkv = low_back(low(matmul(low(first_out), w_self_qkv[half])))
        self_res = attention(self_qkv[:, :D], self_qkv[:, D:2 * D], self_qkv[:, 2 * D:], same_doc & (valid[half] > 0.5)[None, :])
        branch = low_back(matmul(low_back(low(self_res)), w_self_out[half]))
        second = layer_norm(first_out + branch, ln_gain[half, 1], ln_bias[half, 1])
        pre_act = low_back(matmul(low(second), w_ffn_in[half]))
        hidden = low(jax.nn.gelu(pre_act, approximate=False))
        branch = low_back(matmul(hidden, w_ffn_out[half]))
        third_out = layer_norm(second + branch, ln_gain[half, 2], ln_bias[half, 2]) * valid[half][:, None]
        thirds.append(third_out)
    sent_third = [low_back(low(thirds[half])) for half in range(2)]
    results = []
    for half in range(2):
        partner = 1 - half
        gate_in = jnp.concatenate([low(thirds[half]), sent_third[partner]], axis=1)
        gate_value = jax.nn.sigmoid(low_back(matmul(gate_in, w_gate[half])) + gate_bias[half])
        mixed = gate_value * thirds[half] + (1.0 - gate_value) * sent_third[partner]
        results.append(valid[half][:, None] * mixed)
    return jnp.stack(results)

def reference(block_features, cotangent, text_counts, visual_counts, w_cross_q, w_cross_kv, w_cross_out, w_self_qkv, w_self_out, w_ffn_in, w_ffn_out, w_gate, ln_gain, ln_bias, gate_bias):
    params = tuple((weight.astype(jnp.float32) for weight in (w_cross_q, w_cross_kv, w_cross_out, w_self_qkv, w_self_out, w_ffn_in, w_ffn_out, w_gate, ln_gain, ln_bias, gate_bias)))

    def by_group(array):
        return array.astype(jnp.float32).reshape(2, N_DOCS, TOK_DEV, D).transpose(1, 0, 2, 3)

    def one_group(totals, group_data):
        inputs, cot_rows, text_row, visual_row = group_data

        def forward(weights, features):
            return group_forward(weights, features, text_row, visual_row)
        combined_out, pull_back = jax.vjp(forward, params, inputs)
        weight_grads, input_grads = pull_back(cot_rows)
        return (jax.tree.map(jnp.add, totals, weight_grads), (combined_out, input_grads))
    zeros_init = tuple((jnp.zeros(weight.shape, jnp.float32) for weight in params))
    totals, (combined_all, grads_rows) = lax.scan(one_group, zeros_init, (by_group(block_features), by_group(cotangent), text_counts, visual_counts))

    def unstack(array):
        return array.transpose(1, 0, 2, 3).reshape(2, N_DOCS * TOK_DEV, D)
    return (unstack(combined_all), unstack(grads_rows), totals[0], totals[1], totals[2], totals[3], totals[4], totals[5], totals[6], totals[7], totals[8], totals[9], totals[10])
```

```python
import jax
import jax.numpy as jnp
from jax import lax
from jax.sharding import PartitionSpec as P

HD = 64


norm_epsilon = 1e-06
masked_value = -1e30


def from_partner(shard, axis, distance):
    return lax.ppermute(shard, axis, [(i, i ^ 1 << distance) for i in range(lax.axis_size(axis))])


def layer_norm(resid, gain, shift):
    center = resid - jnp.mean(resid, axis=-1, keepdims=True)
    spread = jnp.mean(center * center, axis=-1, keepdims=True)
    return center * lax.rsqrt(spread + norm_epsilon) * gain + shift


def gelu_exact(values):
    return jax.nn.gelu(values, approximate=False)


def times_transposed(left, right):
    return lax.dot_general(
        left, right, (((1,), (1,)), ((), ())), preferred_element_type=jnp.float32
    )


def outer_sum(left, right):
    return lax.dot_general(
        left, right, (((0,), (0,)), ((), ())), preferred_element_type=jnp.float32
    )


def bit_of(index, bit):
    return (index >> bit) & 1


def take_half(stacked, axis, which):
    return lax.dynamic_index_in_dim(stacked, which, axis, keepdims=False)


def reduce_pair_columns(left, right):
    index = lax.axis_index("docs")
    core = bit_of(index, 0)
    width = right.shape[1] // 2
    sent = outer_sum(left, lax.dynamic_slice_in_dim(right, (1 - core) * width, width, 1))
    received = from_partner(sent.astype(jnp.bfloat16), "docs", 0)
    kept = outer_sum(left, lax.dynamic_slice_in_dim(right, core * width, width, 1))
    return kept + received.astype(jnp.float32)


def reduce_rows(half, bits):
    doc_count = lax.axis_size("docs")
    index = lax.axis_index("docs")
    levels = doc_count.bit_length() - 1
    names = list(range(levels - 1, 0, -1))
    rows = half.shape[0] // doc_count
    part = half.reshape((2,) * len(names) + (2 * rows, half.shape[1]))
    for bit in bits:
        axis = names.index(bit)
        mine = bit_of(index, bit)
        sent = take_half(part, axis, 1 - mine).astype(jnp.bfloat16)
        received = from_partner(sent, "docs", bit)
        part = take_half(part, axis, mine) + received.astype(jnp.float32)
        names.pop(axis)
    core = bit_of(index, 0)
    part = part.reshape(2, rows, half.shape[1])
    received = from_partner(take_half(part, 0, 1 - core).astype(jnp.bfloat16), "docs", 0)
    own = take_half(part, 0, core)
    other = received.astype(jnp.float32)
    return jnp.concatenate(
        [jnp.where(core == 0, own, other), jnp.where(core == 0, other, own)], axis=1
    )


def bit_order(first):
    levels = lax.axis_size("docs").bit_length() - 1
    near = list(range(1, levels))
    return near if first == 0 else near[1:] + near[:1]


def summed_gradient(left, right, first=0):
    return reduce_rows(reduce_pair_columns(left, right), bit_order(first))


def layout(text_row, visual_row, tokens):
    order = jnp.arange(text_row.shape[0], dtype=jnp.int32)
    doc_ends = jnp.sum(jnp.where(order[None, :] <= order[:, None], text_row[None, :], 0), axis=1)
    doc_starts = doc_ends - text_row
    positions = jnp.arange(tokens, dtype=jnp.int32)
    doc_ids = jnp.sum((positions[:, None] >= doc_ends[None, :]).astype(jnp.int32), axis=1)
    member = doc_ids[:, None] == order[None, :]
    row_start = jnp.sum(jnp.where(member, doc_starts[None, :], 0), axis=1)
    row_visual = jnp.sum(jnp.where(member, visual_row[None, :], 0), axis=1)
    visible = positions - row_start < row_visual
    return (doc_ids, visible)


def split_heads(rows):
    return rows.reshape(rows.shape[0], rows.shape[1] // HD, HD)


def block_scores(query_block, key_heads, doc_ids, key_valid):
    allowed = (doc_ids[:, None] == doc_ids[None, :]) & key_valid[None, :]
    raw = jnp.einsum(
        "qhd,khd->hqk", query_block, key_heads, preferred_element_type=jnp.float32
    ) * HD ** (-0.5)
    return jnp.where(allowed[None], raw, masked_value)


def attend(queries, key_rows, value_rows, doc_ids, key_valid):
    tokens = queries.shape[0]
    query_heads = split_heads(queries)
    key_heads = split_heads(key_rows)
    value_heads = split_heads(value_rows)
    scores = block_scores(query_heads, key_heads, doc_ids, key_valid)
    row_max = jnp.max(scores, axis=-1, keepdims=True)
    shifted = jnp.exp(scores - row_max)
    row_total = jnp.sum(shifted, axis=-1, keepdims=True)
    attn_probs = (shifted / row_total).astype(jnp.bfloat16)
    results = jnp.einsum(
        "hqk,khd->qhd", attn_probs, value_heads, preferred_element_type=jnp.float32
    )
    return (results.reshape(tokens, -1), row_max + jnp.log(row_total))


def attend_back(queries, key_rows, value_rows, out_grad, log_sums, doc_ids, key_valid):
    tokens = queries.shape[0]
    query_heads = split_heads(queries)
    key_heads = split_heads(key_rows)
    value_heads = split_heads(value_rows)
    out_heads = split_heads(out_grad)
    score_scale = HD ** (-0.5)
    scores = block_scores(query_heads, key_heads, doc_ids, key_valid)
    attn_probs = jnp.exp(scores - log_sums)
    prob_grad = jnp.einsum(
        "qhd,khd->hqk", out_heads, value_heads, preferred_element_type=jnp.float32
    )
    inner = jnp.sum(attn_probs * prob_grad, axis=-1, keepdims=True)
    score_grad = (attn_probs * (prob_grad - inner)).astype(jnp.bfloat16)
    query_grad = (
        jnp.einsum("hqk,khd->qhd", score_grad, key_heads, preferred_element_type=jnp.float32)
        * score_scale
    )
    key_grad = (
        jnp.einsum("hqk,qhd->khd", score_grad, query_heads, preferred_element_type=jnp.float32)
        * score_scale
    )
    value_grad = jnp.einsum(
        "hqk,qhd->khd",
        attn_probs.astype(jnp.bfloat16),
        out_heads,
        preferred_element_type=jnp.float32,
    )
    return (
        query_grad.reshape(tokens, -1),
        key_grad.reshape(tokens, -1),
        value_grad.reshape(tokens, -1),
    )


def body(
    block_features,
    cotangent,
    text_counts,
    visual_counts,
    w_cross_q,
    w_cross_kv,
    w_cross_out,
    w_self_qkv,
    w_self_out,
    w_ffn_in,
    w_ffn_out,
    w_gate,
    ln_gain,
    ln_bias,
    gate_bias,
):
    features = block_features[0]
    cot_rows = cotangent[0].astype(jnp.float32)
    tokens = features.shape[0]
    model_width = features.shape[1]
    half_index = lax.axis_index("stream")
    doc_ids, visible = layout(text_counts[0], visual_counts[0], tokens)
    visible_float = visible.astype(jnp.float32)
    own_valid = jnp.where(half_index == 0, jnp.ones_like(visible_float), visible_float)
    other_valid = jnp.where(half_index == 0, visible_float, jnp.ones_like(visible_float))
    own_keys = own_valid > 0.5
    other_keys = other_valid > 0.5
    cross_q = w_cross_q[0]
    cross_kv = w_cross_kv[0]
    cross_out = w_cross_out[0]
    self_qkv_w = w_self_qkv[0]
    self_out_w = w_self_out[0]
    ffn_in = w_ffn_in[0]
    ffn_out = w_ffn_out[0]
    gate_w = w_gate[0]
    gains = ln_gain[0].astype(jnp.float32)
    shifts = ln_bias[0].astype(jnp.float32)
    gate_shift = gate_bias[0].astype(jnp.float32)
    own_kv = jnp.dot(features, cross_kv, preferred_element_type=jnp.float32).astype(jnp.bfloat16)
    partner_kv = from_partner(own_kv, "stream", 0)
    queries = jnp.dot(features, cross_q, preferred_element_type=jnp.float32).astype(jnp.bfloat16)
    cross_res, cross_sums = attend(
        queries, partner_kv[:, :model_width], partner_kv[:, model_width:], doc_ids, other_keys
    )
    cross_low = cross_res.astype(jnp.bfloat16)
    first_in = features.astype(jnp.float32) + jnp.dot(
        cross_low, cross_out, preferred_element_type=jnp.float32
    )
    first_out, first_pull = jax.vjp(layer_norm, first_in, gains[0], shifts[0])
    first_low = first_out.astype(jnp.bfloat16)
    self_qkv = jnp.dot(first_low, self_qkv_w, preferred_element_type=jnp.float32).astype(
        jnp.bfloat16
    )
    self_queries = self_qkv[:, :model_width]
    self_keys = self_qkv[:, model_width : 2 * model_width]
    self_values = self_qkv[:, 2 * model_width :]
    self_res, self_sums = attend(self_queries, self_keys, self_values, doc_ids, own_keys)
    self_low = self_res.astype(jnp.bfloat16)
    second_in = first_out + jnp.dot(self_low, self_out_w, preferred_element_type=jnp.float32)
    second, second_pull = jax.vjp(layer_norm, second_in, gains[1], shifts[1])
    second_low = second.astype(jnp.bfloat16)
    pre_act = jnp.dot(second_low, ffn_in, preferred_element_type=jnp.float32)
    activated, gelu_pull = jax.vjp(gelu_exact, pre_act)
    hidden = activated.astype(jnp.bfloat16)
    third_in = second + jnp.dot(hidden, ffn_out, preferred_element_type=jnp.float32)
    third_raw, third_pull = jax.vjp(layer_norm, third_in, gains[2], shifts[2])
    third_out = third_raw * own_valid[:, None]
    third_low = third_out.astype(jnp.bfloat16)
    partner_third = from_partner(third_low, "stream", 0)
    gate_in = jnp.concatenate([third_low, partner_third], axis=1)
    gate_value = jax.nn.sigmoid(
        jnp.dot(gate_in, gate_w, preferred_element_type=jnp.float32) + gate_shift
    )
    partner_float = partner_third.astype(jnp.float32)
    combined = own_valid[:, None] * (gate_value * third_out + (1.0 - gate_value) * partner_float)
    out_grad = cot_rows * own_valid[:, None]
    gate_grad = out_grad * (third_out - partner_float)
    logit_grad = gate_grad * gate_value * (1.0 - gate_value)
    grad_gate_shift = jnp.sum(logit_grad, axis=0)
    logit_low = logit_grad.astype(jnp.bfloat16)
    summed_gate_w = summed_gradient(gate_in, logit_low)
    gate_in_grad = times_transposed(logit_low, gate_w)
    partner_grad = gate_in_grad[:, model_width:] + out_grad * (1.0 - gate_value)
    returned_third = from_partner(partner_grad.astype(jnp.bfloat16), "stream", 0)
    third_grad = (
        out_grad * gate_value + gate_in_grad[:, :model_width] + returned_third.astype(jnp.float32)
    ) * own_valid[:, None]
    third_in_grad, gain_grad_c, shift_grad_c = third_pull(third_grad)
    third_in_low = third_in_grad.astype(jnp.bfloat16)
    summed_ffn_out = summed_gradient(hidden, third_in_low)
    hidden_grad = times_transposed(third_in_low, ffn_out)
    (pre_grad,) = gelu_pull(hidden_grad)
    pre_low = pre_grad.astype(jnp.bfloat16)
    summed_ffn_in = summed_gradient(second_low, pre_low)
    second_grad = third_in_grad + times_transposed(pre_low, ffn_in)
    second_in_grad, gain_grad_b, shift_grad_b = second_pull(second_grad)
    second_in_low = second_in_grad.astype(jnp.bfloat16)
    summed_self_out = summed_gradient(self_low, second_in_low, 1)
    self_res_grad = times_transposed(second_in_low, self_out_w).astype(jnp.bfloat16)
    self_q_grad, self_k_grad, self_v_grad = attend_back(
        self_queries, self_keys, self_values, self_res_grad, self_sums, doc_ids, own_keys
    )
    qkv_low = jnp.concatenate([self_q_grad, self_k_grad, self_v_grad], axis=1).astype(jnp.bfloat16)
    summed_self_qkv = summed_gradient(first_low, qkv_low, 1)
    first_grad = second_in_grad + times_transposed(qkv_low, self_qkv_w)
    first_in_grad, gain_grad_a, shift_grad_a = first_pull(first_grad)
    first_in_low = first_in_grad.astype(jnp.bfloat16)
    summed_cross_out = summed_gradient(cross_low, first_in_low)
    cross_res_grad = times_transposed(first_in_low, cross_out).astype(jnp.bfloat16)
    cross_q_grad, partner_k_grad, partner_v_grad = attend_back(
        queries,
        partner_kv[:, :model_width],
        partner_kv[:, model_width:],
        cross_res_grad,
        cross_sums,
        doc_ids,
        other_keys,
    )
    partner_kv_grad = jnp.concatenate([partner_k_grad, partner_v_grad], axis=1).astype(jnp.bfloat16)
    returned_kv = from_partner(partner_kv_grad, "stream", 0)
    cross_q_low = cross_q_grad.astype(jnp.bfloat16)
    summed_cross_q = summed_gradient(features, cross_q_low)
    summed_cross_kv = summed_gradient(features, returned_kv)
    feature_grad = (
        first_in_grad
        + times_transposed(cross_q_low, cross_q)
        + times_transposed(returned_kv, cross_kv)
    )
    gain_grads = jnp.stack([gain_grad_a, gain_grad_b, gain_grad_c])
    shift_grads = jnp.stack([shift_grad_a, shift_grad_b, shift_grad_c])
    small_rows = jnp.concatenate([gain_grads, shift_grads, grad_gate_shift[None]], axis=0)
    gathered = lax.all_gather(small_rows, "docs")
    summed_rows = lax.dynamic_slice_in_dim(
        jnp.sum(gathered, axis=0),
        lax.axis_index("docs") * (model_width // lax.axis_size("docs")),
        model_width // lax.axis_size("docs"),
        1,
    )
    return (
        combined[None],
        feature_grad[None],
        summed_cross_q[None],
        summed_cross_kv[None],
        summed_cross_out[None],
        summed_self_qkv[None],
        summed_self_out[None],
        summed_ffn_in[None],
        summed_ffn_out[None],
        summed_gate_w[None],
        summed_rows[None, 0:3],
        summed_rows[None, 3:6],
        summed_rows[None, 6],
    )


def solution(mesh):
    in_specs = (
        P("stream", "docs", None),
        P("stream", "docs", None),
        P("docs", None),
        P("docs", None),
        P("stream", None, None),
        P("stream", None, None),
        P("stream", None, None),
        P("stream", None, None),
        P("stream", None, None),
        P("stream", None, None),
        P("stream", None, None),
        P("stream", None, None),
        P("stream", None, None),
        P("stream", None, None),
        P("stream", None),
    )
    out_specs = (
        P("stream", "docs", None),
        P("stream", "docs", None),
        P("stream", "docs", None),
        P("stream", "docs", None),
        P("stream", "docs", None),
        P("stream", "docs", None),
        P("stream", "docs", None),
        P("stream", "docs", None),
        P("stream", "docs", None),
        P("stream", "docs", None),
        P("stream", None, "docs"),
        P("stream", None, "docs"),
        P("stream", "docs"),
    )
    return jax.shard_map(body, mesh=mesh, in_specs=in_specs, out_specs=out_specs, check_vma=False)
```

```python
import functools

import jax
import jax.numpy as jnp
from jax import lax
from jax.experimental import pallas as pl
from jax.experimental.pallas import tpu as pltpu
from jax.sharding import PartitionSpec as P

HD = 64
PAIR = 2 * HD
SLOT = 96
FF_BLOCK = 512
VMEM_LIMIT = 60 << 20
F32 = jnp.float32
BF16 = jnp.bfloat16
norm_epsilon = 1e-06
masked_value = -1e30

VM = pltpu.VMEM
SM = pltpu.SMEM
HBM = pl.ANY


def nn(left, right):
    return lax.dot_general(left, right, (((1,), (0,)), ((), ())), preferred_element_type=F32)


def nt(left, right):
    return lax.dot_general(left, right, (((1,), (1,)), ((), ())), preferred_element_type=F32)


def padded_bytes(shape, dtype):
    size = jnp.dtype(dtype).itemsize
    shape = (1,) * (2 - len(shape)) + tuple(shape)
    tile = 32 // size
    total = -(-shape[-1] // 128) * 128 * -(-shape[-2] // tile) * tile * size
    for extent in shape[:-2]:
        total *= extent
    return total


def run_kernel(kernel, name, ins, outs, scratch=(), us=5.0, spare=6 << 20):
    need = sum(padded_bytes(array.shape, array.dtype) for array, space in ins if space is VM)
    need += sum(padded_bytes(shape, dtype) for shape, dtype, space in outs if space is VM)
    need += sum(
        padded_bytes(ref.shape, ref.dtype) for ref in scratch if hasattr(ref, "memory_space")
        and ref.memory_space == VM
    )
    return pl.pallas_call(
        kernel,
        name=name,
        in_specs=[pl.BlockSpec(memory_space=space) for _, space in ins],
        out_specs=[pl.BlockSpec(memory_space=space) for _, _, space in outs],
        out_shape=[jax.ShapeDtypeStruct(shape, dtype) for shape, dtype, _ in outs],
        scratch_shapes=list(scratch),
        compiler_params=pltpu.CompilerParams(vmem_limit_bytes=min(VMEM_LIMIT, need + spare)),
        cost_estimate=pl.CostEstimate(
            flops=int(us * 30e9), bytes_accessed=1000, transcendentals=0
        ),
    )(*[array for array, _ in ins])


def fetch(source, target, sem):
    copy = pltpu.make_async_copy(source, target, sem)
    copy.start()
    return copy


def normalise(resid):
    center = resid - jnp.mean(resid, axis=-1, keepdims=True)
    scale = lax.rsqrt(jnp.mean(center * center, axis=-1, keepdims=True) + norm_epsilon)
    return center * scale, scale


def normalise_back(grad, unit, scale, gain):
    gain_sum = jnp.sum(grad * unit, axis=0, keepdims=True)
    shift_sum = jnp.sum(grad, axis=0, keepdims=True)
    scaled = grad * gain
    first = jnp.mean(scaled, axis=-1, keepdims=True)
    second = jnp.mean(scaled * unit, axis=-1, keepdims=True)
    return scale * (scaled - first - unit * second), gain_sum, shift_sum


def attend(q_ref, q_at, k_ref, k_at, v_ref, v_at, bias_ref, out_ref, probs_ref):
    def step(pair, carry):
        at = pair * PAIR
        queries = q_ref[:, pl.ds(pl.multiple_of(q_at + at, PAIR), PAIR)] * jnp.asarray(
            HD**-0.5, BF16
        )
        keys = k_ref[:, pl.ds(pl.multiple_of(k_at + at, PAIR), PAIR)]
        values = v_ref[:, pl.ds(pl.multiple_of(v_at + at, PAIR), PAIR)].T
        first = lax.broadcasted_iota(jnp.int32, keys.shape, 1) < HD
        zero = jnp.zeros_like(keys)
        mixed = []
        for head in range(2):
            own = jnp.where(first, keys, zero) if head == 0 else jnp.where(first, zero, keys)
            scores = nt(own, queries) + bias_ref[...]
            shifted = jnp.exp(scores - jnp.max(scores, axis=0, keepdims=True))
            probs = (shifted * (1.0 / jnp.sum(shifted, axis=0, keepdims=True))).astype(BF16)
            probs_ref[2 * pair + head] = probs
            mixed.append(nn(values[head * HD : (head + 1) * HD], probs))
        out_ref[:, pl.ds(pl.multiple_of(at, PAIR), PAIR)] = (
            jnp.concatenate(mixed, axis=0).astype(BF16).T
        )
        return carry

    lax.fori_loop(0, out_ref.shape[1] // PAIR, step, 0)


def attend_back(
    q_ref, q_at, k_ref, k_at, v_ref, v_at, mixed_ref, grad_ref, probs_ref,
    dq_ref, dq_at, dk_ref, dk_at, dv_ref, dv_at,
):
    def step(pair, carry):
        at = pair * PAIR

        def columns(ref, start):
            return ref[:, pl.ds(pl.multiple_of(start + at, PAIR), PAIR)]

        queries = columns(q_ref, q_at)
        keys = columns(k_ref, k_at)
        values = columns(v_ref, v_at)
        grads = columns(grad_ref, 0)
        first = lax.broadcasted_iota(jnp.int32, keys.shape, 1) < HD
        zero = jnp.zeros_like(values)
        grads_t = grads.T
        keys_t = keys.T
        inner = grads_t.astype(F32) * columns(mixed_ref, 0).T.astype(F32)
        key_grads, value_grads, query_grads = [], [], []
        for head in range(2):
            rows = slice(head * HD, (head + 1) * HD)
            own = jnp.where(first, values, zero) if head == 0 else jnp.where(first, zero, values)
            probs = probs_ref[2 * pair + head]
            score_grad = probs.astype(F32) * (
                nn(own, grads_t) - jnp.sum(inner[rows], axis=0, keepdims=True)
            )
            score_grad = score_grad.astype(BF16)
            key_grads.append(nn(score_grad, queries))
            value_grads.append(nn(probs, grads))
            query_grads.append(nn(keys_t[rows], score_grad))
        scale = HD**-0.5

        def store(ref, start, value):
            ref[:, pl.ds(pl.multiple_of(start + at, PAIR), PAIR)] = value

        store(dk_ref, dk_at, (jnp.where(first, key_grads[0], key_grads[1]) * scale).astype(BF16))
        store(dv_ref, dv_at, jnp.where(first, value_grads[0], value_grads[1]).astype(BF16))
        store(dq_ref, dq_at, (jnp.concatenate(query_grads, axis=0) * scale).astype(BF16).T)
        return carry

    lax.fori_loop(0, grad_ref.shape[1] // PAIR, step, 0)


def set_bias(bias_ref, key_doc_ref, query_doc_ref):
    bias_ref[...] = jnp.where(key_doc_ref[...] == query_doc_ref[...], 0.0, masked_value)


def put_split(split, core, value, at, sent_ref, kept_ref):
    cols = pl.ds(at, value.shape[1])
    if not split:
        kept_ref[:, cols] = value.astype(BF16)
        return
    groups, piece = kept_ref.shape[:2]
    pieces = value.reshape(groups, 2, piece, value.shape[1]).astype(BF16)
    even = core == 0
    kept_ref[:, :, cols] = jnp.where(even, pieces[:, 0], pieces[:, 1])
    sent_ref[:, :, cols] = jnp.where(even, pieces[:, 1], pieces[:, 0])


def query_kernel(where, feat, pick, wq_hbm, x_out, q_out, q_sent, wq, sem):
    packed = pick.shape[0]
    copy = fetch(wq_hbm, wq, sem)

    @pl.when(where[0] == 0)
    def _():
        x_out[...] = feat[...]

    @pl.when(where[0] != 0)
    def _():
        x_out[:packed] = nn(pick[...], feat[...]).astype(BF16)
        x_out[packed:] = jnp.zeros((x_out.shape[0] - packed, x_out.shape[1]), BF16)

    copy.wait()
    q_out[...] = nn(x_out[...], wq[...]).astype(BF16)
    q_sent[...] = q_out[:packed]


def key_value_kernel(x, w, kv_out, kv_sent):
    kv_out[...] = nn(x[...], w[...]).astype(BF16)
    kv_sent[...] = kv_out[: kv_sent.shape[0]]


def vision_attend_kernel(where, q, kv, query_doc, key_doc, mixed, probs, bias):
    width = q.shape[1]

    @pl.when(where[0] == 0)
    def _():
        set_bias(bias, key_doc, query_doc)
        attend(q, 0, kv, 0, kv, width, bias, mixed, probs)


def middle_kernel(
    where, x, q, kv, vision_mixed, pick, cross_query, cross_key, self_query, self_key, valid,
    gains, shifts, wo_hbm, wqkv_hbm, ws_hbm, wi_hbm, wf_hbm,
    mixed_hbm, cross_probs_hbm, first_low_hbm, unit1_hbm, scale1_hbm, qkv_hbm, self_low_hbm,
    self_probs_hbm, second_low_hbm, unit2_hbm, scale2_hbm, hidden_hbm, slope_hbm, unit3_hbm,
    scale3_hbm, third_hbm, third_low_hbm, third_sent_hbm,
    wo, wqkv, ws, wi, wf, mixed, cross_probs, first_low, unit1, scale1, qkv, self_low,
    self_probs, second_low, unit2, scale2, hidden, slope, unit3, scale3, third, third_low,
    third_sent, first, cross_bias, self_bias, load_sem, save_sem,
):
    width = x.shape[1]
    packed = kv.shape[0]
    loads = [
        fetch(source, target, load_sem.at[i])
        for i, (source, target) in enumerate(
            ((wo_hbm, wo), (wqkv_hbm, wqkv), (ws_hbm, ws), (wi_hbm, wi), (wf_hbm, wf))
        )
    ]
    saves = []

    def save(source, target):
        saves.append(fetch(source, target, save_sem.at[len(saves)]))

    gain = gains[...].astype(F32)
    shift = shifts[...].astype(F32)

    @pl.when(where[0] == 0)
    def _():
        set_bias(cross_bias, cross_key, cross_query)
        attend(q, 0, kv, 0, kv, width, cross_bias, mixed, cross_probs)

    @pl.when(where[0] != 0)
    def _():
        mixed[:packed] = vision_mixed[...]
        mixed[packed:] = jnp.zeros((mixed.shape[0] - packed, width), BF16)

    save(mixed, mixed_hbm)
    save(cross_probs, cross_probs_hbm)
    set_bias(self_bias, self_key, self_query)
    loads[0].wait()
    unit, scale = normalise(x[...].astype(F32) + nn(mixed[...], wo[...]))
    unit1[...] = unit.astype(BF16)
    scale1[...] = jnp.broadcast_to(scale, scale1.shape)
    first[...] = unit * gain[0:1] + shift[0:1]
    first_low[...] = first[...].astype(BF16)
    save(unit1, unit1_hbm)
    save(scale1, scale1_hbm)
    save(first_low, first_low_hbm)
    loads[1].wait()
    qkv[...] = nn(first_low[...], wqkv[...]).astype(BF16)
    save(qkv, qkv_hbm)
    attend(qkv, 0, qkv, width, qkv, 2 * width, self_bias, self_low, self_probs)
    save(self_low, self_low_hbm)
    save(self_probs, self_probs_hbm)
    loads[2].wait()
    unit, scale = normalise(first[...] + nn(self_low[...], ws[...]))
    unit2[...] = unit.astype(BF16)
    scale2[...] = jnp.broadcast_to(scale, scale2.shape)
    third[...] = unit * gain[1:2] + shift[1:2]
    second_low[...] = third[...].astype(BF16)
    save(unit2, unit2_hbm)
    save(scale2, scale2_hbm)
    save(second_low, second_low_hbm)
    loads[3].wait()
    loads[4].wait()

    def ffn(block, carry):
        cols = pl.ds(pl.multiple_of(block * FF_BLOCK, FF_BLOCK), FF_BLOCK)
        pre = nn(second_low[...], wi[:, cols])
        below = 0.5 * (1.0 + lax.erf(pre * (2.0**-0.5)))
        density = jnp.exp(pre * pre * -0.5) * 0.3989422804014327
        active = (pre * below).astype(BF16)
        hidden[:, cols] = active
        slope[:, cols] = (below + pre * density).astype(BF16)
        third[...] += nn(active, wf[cols, :])
        return carry

    lax.fori_loop(0, hidden.shape[1] // FF_BLOCK, ffn, 0)
    save(hidden, hidden_hbm)
    save(slope, slope_hbm)
    unit, scale = normalise(third[...])
    unit3[...] = unit.astype(BF16)
    scale3[...] = jnp.broadcast_to(scale, scale3.shape)
    third[...] = (unit * gain[2:3] + shift[2:3]) * valid[...]
    third_low[...] = third[...].astype(BF16)

    @pl.when(where[0] == 0)
    def _():
        third_sent[...] = nn(pick[...], third_low[...]).astype(BF16)

    @pl.when(where[0] != 0)
    def _():
        third_sent[...] = third_low[:packed]

    save(third_sent, third_sent_hbm)
    save(third_low, third_low_hbm)
    save(third, third_hbm)
    save(unit3, unit3_hbm)
    save(scale3, scale3_hbm)
    for copy in saves:
        copy.wait()


def gate_kernel(
    where, third, third_low, other, pick, pick_t, valid, cot, bias, wg_hbm,
    combined, other_low, logit_low, own_part, sent, bias_sum, wg, cot_rows, sem,
):
    width = third.shape[1]
    packed = pick.shape[0]
    rows = third.shape[0]
    copy = fetch(wg_hbm, wg, sem)

    @pl.when(where[0] == 0)
    def _():
        other_low[...] = nn(pick_t[...], other[...]).astype(BF16)
        cot_rows[...] = cot[...]

    @pl.when(where[0] != 0)
    def _():
        other_low[:packed] = other[...]
        other_low[packed:] = jnp.zeros((rows - packed, width), BF16)
        cot_rows[:packed] = nn(pick[...], cot[...]).astype(BF16)
        cot_rows[packed:] = jnp.zeros((rows - packed, width), BF16)

    copy.wait()
    logits = nn(third_low[...], wg[:width]) + nn(other_low[...], wg[width:])
    gate = jax.nn.sigmoid(logits + bias[...].astype(F32))
    other_rows = other_low[...].astype(F32)
    out_grad = cot_rows[...].astype(F32) * valid[...]
    mixed = valid[...] * (gate * third[...] + (1.0 - gate) * other_rows)

    @pl.when(where[0] == 0)
    def _():
        combined[...] = mixed

    @pl.when(where[0] != 0)
    def _():
        high = mixed[:packed].astype(BF16)
        rest = (mixed[:packed] - high.astype(F32)).astype(BF16)
        combined[...] = nn(pick_t[...], high) + nn(pick_t[...], rest)

    logit_grad = out_grad * (third[...] - other_rows) * gate * (1.0 - gate)
    bias_sum[...] = jnp.sum(logit_grad, axis=0, keepdims=True)
    logit_low[...] = logit_grad.astype(BF16)
    own_part[...] = nt(logit_low[...], wg[:width]) + out_grad * gate
    partner = (nt(logit_low[...], wg[width:]) + out_grad * (1.0 - gate)).astype(BF16)

    @pl.when(where[0] == 0)
    def _():
        sent[...] = nn(pick[...], partner).astype(BF16)

    @pl.when(where[0] != 0)
    def _():
        sent[...] = partner[:packed]


def gate_weight_kernel(split, where, own, other, grad, *outs):
    sent, kept = outs if split else (None,) + outs
    half = own.shape[1]
    full = kept.shape[0] * kept.shape[1] * 2 if split else kept.shape[0]
    for part, left in enumerate((own, other)):
        value = nn(left[...].T, grad[...])
        if split:
            rows = kept.shape[0] * half // full
            put_split(
                split, where[1], value, 0,
                sent.at[pl.ds(part * rows, rows)], kept.at[pl.ds(part * rows, rows)],
            )
        else:
            kept[pl.ds(part * half, half)] = value.astype(BF16)


def third_back_kernel(
    split, where, own_part, returned, pick_t, valid, unit, scale, gains, hidden_hbm, *rest
):
    if split:
        grad_out, low_out, sums, sent, kept, grad, hidden, sem = rest
    else:
        grad_out, low_out, sums, kept, grad, hidden, sem = rest
    packed = returned.shape[0]
    copy = fetch(hidden_hbm, hidden, sem)
    grad[...] = own_part[...]

    @pl.when(where[0] == 0)
    def _():
        grad[...] += nn(pick_t[...], returned[...])

    @pl.when(where[0] != 0)
    def _():
        grad[:packed] += returned[...].astype(F32)

    value, gain_sum, shift_sum = normalise_back(
        grad[...] * valid[...], unit[...].astype(F32), scale[:, 0:1], gains[2:3].astype(F32)
    )
    grad_out[...] = value
    low_out[...] = value.astype(BF16)
    sums[0:1] = gain_sum
    sums[1:2] = shift_sum
    copy.wait()
    if split:
        groups, piece = kept.shape[:2]
        even = where[1] == 0
        for group in range(groups):
            left = hidden[:, group * 2 * piece : (group + 1) * 2 * piece].T
            value = nn(left, low_out[...]).astype(BF16)
            kept[group] = jnp.where(even, value[:piece], value[piece:])
            sent[group] = jnp.where(even, value[piece:], value[:piece])
    else:
        for at in range(0, hidden.shape[1], FF_BLOCK):
            left = hidden[:, at : at + FF_BLOCK].T
            kept[at : at + FF_BLOCK] = nn(left, low_out[...]).astype(BF16)


def ffn_back_kernel(
    split, where, third_grad, third_low, slope, second_low, unit, scale, gains, wi_hbm, wf_hbm,
    *rest,
):
    if split:
        grad_out, low_out, sums, sent, kept, wi, wf, left, total, sem = rest
    else:
        grad_out, low_out, sums, kept, wi, wf, left, total, sem = rest
        sent = None
    copies = [fetch(wf_hbm, wf, sem.at[0]), fetch(wi_hbm, wi, sem.at[1])]
    left[...] = second_low[...].T
    total[...] = third_grad[...]
    for copy in copies:
        copy.wait()

    def step(block, carry):
        at = pl.multiple_of(block * FF_BLOCK, FF_BLOCK)
        cols = pl.ds(at, FF_BLOCK)
        back = nt(third_low[...], wf[cols, :])
        pre_low = (back * slope[:, cols].astype(F32)).astype(BF16)
        total[...] += nt(pre_low, wi[:, cols])
        put_split(split, where[1], nn(left[...], pre_low), at, sent, kept)
        return carry

    lax.fori_loop(0, wi.shape[1] // FF_BLOCK, step, 0)
    value, gain_sum, shift_sum = normalise_back(
        total[...], unit[...].astype(F32), scale[:, 0:1], gains[1:2].astype(F32)
    )
    grad_out[...] = value
    low_out[...] = value.astype(BF16)
    sums[0:1] = gain_sum
    sums[1:2] = shift_sum


def self_back_kernel(
    second_grad, second_low, qkv, self_low, unit, scale, gains, probs_hbm, ws_hbm, wqkv_hbm, wo_hbm,
    dqkv, grad_out, low_out, cross, cross_sent, sums, probs, ws, wqkv, wo, mixed_grad, sem,
):
    width = second_grad.shape[1]
    copies = [
        fetch(source, target, sem.at[i])
        for i, (source, target) in enumerate(
            ((ws_hbm, ws), (probs_hbm, probs), (wqkv_hbm, wqkv), (wo_hbm, wo))
        )
    ]
    copies[0].wait()
    mixed_grad[...] = nt(second_low[...], ws[...]).astype(BF16)
    copies[1].wait()
    attend_back(
        qkv, 0, qkv, width, qkv, 2 * width, self_low, mixed_grad, probs,
        dqkv, 0, dqkv, width, dqkv, 2 * width,
    )
    copies[2].wait()
    value, gain_sum, shift_sum = normalise_back(
        second_grad[...] + nt(dqkv[...], wqkv[...]),
        unit[...].astype(F32),
        scale[:, 0:1],
        gains[0:1].astype(F32),
    )
    grad_out[...] = value
    low_out[...] = value.astype(BF16)
    sums[0:1] = gain_sum
    sums[1:2] = shift_sum
    copies[3].wait()
    cross[...] = nt(low_out[...], wo[...]).astype(BF16)
    cross_sent[...] = cross[: cross_sent.shape[0]]


def self_weight_kernel(
    split, where, self_low, second_grad, first_low, dqkv, mixed, first_grad, *outs
):
    sent, kept = outs if split else (None,) + outs
    width = self_low.shape[1]
    put_split(split, where[1], nn(self_low[...].T, second_grad[...]), 0, sent, kept)
    left = first_low[...].T
    for part in range(3):
        value = nn(left, dqkv[:, part * width : (part + 1) * width])
        put_split(split, where[1], value, (1 + part) * width, sent, kept)
    put_split(split, where[1], nn(mixed[...].T, first_grad[...]), 4 * width, sent, kept)


def vision_back_kernel(where, q, kv, mixed, grad, probs, own, sent):
    width = q.shape[1]

    @pl.when(where[0] == 0)
    def _():
        attend_back(
            q, 0, kv, 0, kv, width, mixed, grad, probs, sent, 0, own, 0, own, width
        )


def cross_back_kernel(where, q, kv, mixed, grad, probs, own, sent):
    width = q.shape[1]

    @pl.when(where[0] == 0)
    def _():
        attend_back(q, 0, kv, 0, kv, width, mixed, grad, probs, own, 0, sent, 0, sent, width)


def cross_weight_kernel(
    split, where, own_query, own_key_value, query, key_value, x, first_sums, second_sums,
    third_sums, bias_sum, *outs,
):
    dqkv, sent, kept = outs if split else (outs[0], None, outs[1])
    width = x.shape[1]
    packed = query.shape[0]

    @pl.when(where[0] == 0)
    def _():
        dqkv[:, :width] = own_query[...]
        dqkv[:, width:] = own_key_value[...]

    @pl.when(where[0] != 0)
    def _():
        dqkv[:packed, :width] = query[...]
        dqkv[:packed, width:] = key_value[...]
        dqkv[packed:] = jnp.zeros((dqkv.shape[0] - packed, dqkv.shape[1]), BF16)

    left = x[...].T
    for part in range(3):
        value = nn(left, dqkv[:, part * width : (part + 1) * width])
        put_split(split, where[1], value, part * width, sent, kept)
    small = jnp.concatenate(
        [first_sums[...], second_sums[...], third_sums[...], bias_sum[...],
         jnp.zeros((121, width), F32)], axis=0,
    )
    put_split(split, where[1], small.T, 3 * width, sent, kept)


def feature_kernel(where, dqkv, first_grad, pick_t, wq_hbm, wkv_hbm, out, wq, wkv, total, sem):
    width = first_grad.shape[1]
    packed = pick_t.shape[1]
    copies = [fetch(wq_hbm, wq, sem.at[0]), fetch(wkv_hbm, wkv, sem.at[1])]
    copies[0].wait()
    copies[1].wait()
    total[...] = (
        first_grad[...] + nt(dqkv[:, :width], wq[...]) + nt(dqkv[:, width:], wkv[...])
    )

    @pl.when(where[0] == 0)
    def _():
        out[...] = total[...]

    @pl.when(where[0] != 0)
    def _():
        value = total[:packed]
        high = value.astype(BF16)
        rest = (value - high.astype(F32)).astype(BF16)
        out[...] = nn(pick_t[...], high) + nn(pick_t[...], rest)


def to_partner(shard):
    return lax.ppermute(shard, "stream", [(0, 1), (1, 0)])


def to_language(shard):
    return lax.ppermute(shard, "stream", [(1, 0)])


def to_vision(shard):
    return lax.ppermute(shard, "stream", [(0, 1)])


def swap(shard, bit):
    count = lax.axis_size("docs")
    return lax.ppermute(shard, "docs", [(i, i ^ 1 << bit) for i in range(count)])


def after(value, *others):
    return lax.optimization_barrier((value,) + others)[0] if others else value


class Summation:
    def __init__(self, parts, order):
        self.index = lax.axis_index("docs")
        count = lax.axis_size("docs")
        self.names = [bit for bit in range(count.bit_length() - 2, 0, -1)]
        self.order = list(order)
        if len(parts) == 2:
            sent, kept = parts
        else:
            full = parts[0].reshape(count // 2, 2, -1, parts[0].shape[-1])
            core = self.index & 1
            sent = lax.dynamic_index_in_dim(full, 1 - core, 1, keepdims=False)
            kept = lax.dynamic_index_in_dim(full, core, 1, keepdims=False)
        self.total = kept.reshape((2,) * len(self.names) + kept.shape[1:])
        self.arrived = swap(sent, 0).reshape(self.total.shape)

    def advance(self, *earlier):
        if self.arrived is None:
            return False
        total = self.total.astype(F32) + after(self.arrived, *earlier).astype(F32)
        if not self.order:
            self.total, self.arrived = total, None
            return False
        bit = self.order.pop(0)
        axis = self.names.index(bit)
        self.names.pop(axis)
        mine = (self.index >> bit) & 1
        sent = lax.dynamic_index_in_dim(total, 1 - mine, axis, keepdims=False).astype(BF16)
        self.total = lax.dynamic_index_in_dim(total, mine, axis, keepdims=False)
        self.sent = sent
        self.arrived = swap(sent, bit)
        return True


def bit_order(first):
    bits = list(range(1, lax.axis_size("docs").bit_length() - 1))
    return bits if first == 0 else bits[1:] + bits[:1]


def layout(text_row, visual_row, tokens, vision):
    docs = text_row.shape[0]
    order = jnp.arange(docs, dtype=jnp.int32)
    ends = jnp.sum(jnp.where(order[None, :] <= order[:, None], text_row[None, :], 0), axis=1)
    starts = ends - text_row
    rows = jnp.arange(tokens, dtype=jnp.int32)
    doc = jnp.sum((rows[:, None] >= ends[None, :]).astype(jnp.int32), axis=1)
    slot = rows // SLOT
    place = rows % SLOT
    member = slot[:, None] == order[None, :]
    seen = place < jnp.sum(jnp.where(member, visual_row[None, :], 0), axis=1)
    target = jnp.where(seen, place + jnp.sum(jnp.where(member, starts[None, :], 0), axis=1), -1)
    slot_key = jnp.where(seen, slot, -1)
    packed = docs * SLOT
    pick = (target[:packed, None] == rows[None, :]).astype(BF16)
    pick_t = (target[None, :packed] == rows[:, None]).astype(BF16)
    own_query = jnp.where(vision, slot, doc)
    own_key = jnp.where(vision, slot_key, doc)
    valid = jnp.where(vision, seen, True).astype(F32)
    return {
        "pick": pick,
        "pick_t": pick_t,
        "doc_row": doc[None, :],
        "doc_column": doc[:, None],
        "slot_row": slot[None, :packed],
        "slot_key": slot_key[:packed, None],
        "self_query": own_query[None, :],
        "self_key": own_key[:, None],
        "valid": valid[:, None],
    }


def body(
    block_features, cotangent, text_counts, visual_counts, w_cross_q, w_cross_kv, w_cross_out,
    w_self_qkv, w_self_out, w_ffn_in, w_ffn_out, w_gate, ln_gain, ln_bias, gate_bias,
):
    feat = block_features[0]
    rows, width = feat.shape
    wq, wkv, wo = w_cross_q[0], w_cross_kv[0], w_cross_out[0]
    wqkv, ws = w_self_qkv[0], w_self_out[0]
    wi, wf, wg = w_ffn_in[0], w_ffn_out[0], w_gate[0]
    gains, shifts = ln_gain[0], ln_bias[0]
    hidden_width = wi.shape[1]
    half = lax.axis_index("stream")
    device = lax.axis_index("docs")
    count = lax.axis_size("docs")
    groups = count // 2
    split = (width // count) % 16 == 0
    lay = layout(text_counts[0], visual_counts[0], rows, half == 1)
    packed = lay["pick"].shape[0]
    heads = width // HD
    where = jnp.stack([half, device & 1]).astype(jnp.int32)
    dma = pltpu.SemaphoreType.DMA

    def weight_outs(total_rows, columns):
        if split:
            shape = (groups, total_rows // count, columns)
            return [(shape, BF16, VM), (shape, BF16, VM)]
        return [((total_rows, columns), BF16, VM)]

    x, q, q_sent = run_kernel(
        query_kernel, "query",
        [(where, SM), (feat, VM), (lay["pick"], VM), (wq, HBM)],
        [((rows, width), BF16, VM), ((rows, width), BF16, VM), ((packed, width), BF16, VM)],
        [VM((width, width), BF16), dma],
    )
    vision_q = to_language(q_sent)
    kv, kv_sent = run_kernel(
        key_value_kernel, "key_value",
        [(after(x, q_sent), VM), (wkv, VM)],
        [((rows, 2 * width), BF16, VM), ((packed, 2 * width), BF16, VM)],
    )
    vision_kv = to_language(kv_sent)
    vision_mixed, vision_probs = run_kernel(
        vision_attend_kernel, "vision_attend",
        [(where, SM), (vision_q, VM), (after(kv, kv_sent), VM), (lay["slot_row"], VM),
         (lay["doc_column"], VM)],
        [((packed, width), BF16, VM), ((heads, rows, packed), BF16, VM)],
        [VM((rows, packed), F32)],
    )
    vision_mixed_here = to_vision(vision_mixed)

    def state(*shape, kind=BF16):
        return (shape, kind, HBM)

    full = state(rows, width)
    lane = state(rows, 128, kind=F32)
    middle_outs = [
        full, state(heads, packed, rows), full, full, lane, state(rows, 3 * width), full,
        state(heads, rows, rows), full, full, lane, state(rows, hidden_width),
        state(rows, hidden_width), full, lane, state(rows, width, kind=F32), full,
        state(packed, width),
    ]
    middle_weights = [wo, wqkv, ws, wi, wf]
    (
        mixed, cross_probs, first_low, unit1, scale1, qkv, self_low, self_probs, second_low, unit2,
        scale2, hidden, slope, unit3, scale3, third, third_low, third_sent,
    ) = run_kernel(
        middle_kernel, "middle",
        [(where, SM), (x, VM), (q, VM), (vision_kv, VM), (vision_mixed_here, VM),
         (lay["pick"], VM), (lay["doc_row"], VM), (lay["slot_key"], VM), (lay["self_query"], VM),
         (lay["self_key"], VM), (lay["valid"], VM), (gains, VM), (shifts, VM)]
        + [(w, HBM) for w in middle_weights],
        middle_outs,
        [VM(w.shape, BF16) for w in middle_weights]
        + [VM(shape, kind) for shape, kind, _ in middle_outs]
        + [VM((rows, width), F32), VM((packed, rows), F32), VM((rows, rows), F32),
           dma((len(middle_weights),)), dma((len(middle_outs),))],
    )
    other = to_partner(third_sent)
    combined, other_low, logit_low, own_part, partner_sent, bias_sum = run_kernel(
        gate_kernel, "gate",
        [(where, SM), (third, VM), (third_low, VM), (other, VM), (lay["pick"], VM),
         (lay["pick_t"], VM), (lay["valid"], VM), (cotangent[0], VM), (gate_bias, VM), (wg, HBM)],
        [((rows, width), F32, VM), ((rows, width), BF16, VM), ((rows, width), BF16, VM),
         ((rows, width), F32, VM), ((packed, width), BF16, VM), ((1, width), F32, VM)],
        [VM(wg.shape, BF16), VM((rows, width), BF16), dma],
    )
    returned = to_partner(partner_sent)
    gate_parts = run_kernel(
        functools.partial(gate_weight_kernel, split), "gate_weight",
        [(where, SM), (third_low, VM), (other_low, VM), (after(logit_low, partner_sent), VM)],
        weight_outs(2 * width, width),
    )
    gate_sum = Summation(gate_parts, bit_order(0))
    gate_sum.advance()
    third_back = run_kernel(
        functools.partial(third_back_kernel, split), "third_back",
        [(where, SM), (own_part, VM), (after(returned, gate_sum.sent), VM), (lay["pick_t"], VM),
         (lay["valid"], VM), (unit3, VM), (scale3, VM), (gains, VM), (hidden, HBM)],
        [((rows, width), F32, VM), ((rows, width), BF16, VM), ((2, width), F32, VM)]
        + weight_outs(hidden_width, width),
        [VM((rows, width), F32), VM((rows, hidden_width), BF16), dma],
    )
    third_grad, third_grad_low, third_sums = third_back[:3]
    out_sum = Summation(third_back[3:], bit_order(1))
    ffn_back = run_kernel(
        functools.partial(ffn_back_kernel, split), "ffn_back",
        [(where, SM), (third_grad, VM), (third_grad_low, VM), (slope, VM), (second_low, VM),
         (unit2, VM), (scale2, VM), (gains, VM), (wi, HBM), (wf, HBM)],
        [((rows, width), F32, VM), ((rows, width), BF16, VM), ((2, width), F32, VM)]
        + weight_outs(width, hidden_width),
        [VM(wi.shape, BF16), VM(wf.shape, BF16), VM((width, rows), BF16), VM((rows, width), F32),
         dma((2,))], us=13.0,
    )
    second_grad, second_grad_low, second_sums = ffn_back[:3]
    in_sum = Summation(ffn_back[3:], bit_order(0))
    out_sum.advance(second_sums)
    gate_sum.advance(second_sums)
    dqkv, first_grad, first_grad_low, cross_grad, cross_grad_sent, first_sums = run_kernel(
        self_back_kernel, "self_back",
        [(second_grad, VM), (after(second_grad_low, out_sum.sent, gate_sum.sent), VM), (qkv, VM),
         (self_low, VM), (unit1, VM),
         (scale1, VM), (gains, VM), (self_probs, HBM), (ws, HBM), (wqkv, HBM), (wo, HBM)],
        [((rows, 3 * width), BF16, VM), ((rows, width), F32, VM), ((rows, width), BF16, VM),
         ((rows, width), BF16, VM), ((packed, width), BF16, VM), ((2, width), F32, VM)],
        [VM((heads, rows, rows), BF16), VM(ws.shape, BF16), VM(wqkv.shape, BF16),
         VM(wo.shape, BF16), VM((rows, width), BF16), dma((4,))], us=15.0,
    )
    vision_grad = to_language(cross_grad_sent)
    in_sum.advance(first_sums)
    gate_sum.advance(first_sums)
    self_parts = run_kernel(
        functools.partial(self_weight_kernel, split), "self_weight",
        [(where, SM), (self_low, VM), (second_grad_low, VM), (first_low, VM),
         (after(dqkv, cross_grad_sent, in_sum.sent, gate_sum.sent), VM), (mixed, VM),
         (first_grad_low, VM)],
        weight_outs(width, 5 * width), us=5.0,
    )
    self_sum = Summation(self_parts, bit_order(0))
    own_key_value, query_sent = run_kernel(
        vision_back_kernel, "vision_back",
        [(where, SM), (vision_q, VM), (kv, VM), (vision_mixed, VM),
         (after(vision_grad, *self_parts), VM), (vision_probs, VM)],
        [((rows, 2 * width), BF16, VM), ((packed, width), BF16, VM)], us=5.0,
    )
    query_here = to_vision(query_sent)
    self_sum.advance(query_sent)
    out_sum.advance(query_sent)
    own_query, key_value_sent = run_kernel(
        cross_back_kernel, "cross_back",
        [(where, SM), (q, VM), (vision_kv, VM), (mixed, VM),
         (after(cross_grad, query_sent, self_sum.sent, out_sum.sent), VM), (cross_probs, VM)],
        [((rows, width), BF16, VM), ((packed, 2 * width), BF16, VM)], us=7.0,
    )
    key_value_here = to_vision(key_value_sent)
    gate_sum.advance(key_value_sent)
    in_sum.advance(key_value_sent)
    cross_parts = run_kernel(
        functools.partial(cross_weight_kernel, split), "cross_weight",
        [(where, SM), (own_query, VM), (own_key_value, VM), (query_here, VM),
         (after(key_value_here, in_sum.sent), VM),
         (x, VM), (first_sums, VM), (second_sums, VM), (third_sums, VM), (bias_sum, VM)],
        [((rows, 3 * width), BF16, VM)] + weight_outs(width, 3 * width + 128), us=3.0,
    )
    cross_sum = Summation(cross_parts[1:], bit_order(1))
    (feature_grad,) = run_kernel(
        feature_kernel, "feature",
        [(where, SM), (after(cross_parts[0], *cross_parts[1:]), VM), (first_grad, VM),
         (lay["pick_t"], VM), (wq, HBM), (wkv, HBM)],
        [((rows, width), F32, VM)],
        [VM(wq.shape, BF16), VM(wkv.shape, BF16), VM((rows, width), F32), dma((2,))], us=4.0,
    )
    cross_sum.advance(feature_grad)
    out_sum.advance(cross_sum.sent)
    in_sum.advance(out_sum.sent)
    self_sum.advance(in_sum.sent)
    cross_sum.advance(self_sum.sent)
    out_sum.advance(cross_sum.sent)
    in_sum.advance(out_sum.total)
    self_sum.advance(in_sum.total)
    cross_sum.advance(self_sum.sent)
    self_sum.advance(cross_sum.sent)
    cross_sum.advance(self_sum.total)
    pending = [gate_sum, out_sum, in_sum, self_sum, cross_sum]
    while pending:
        pending = [one for one in pending if one.advance()]
    piece = width // count
    gate_w, out_w, in_w = gate_sum.total, out_sum.total, in_sum.total
    self_w, cross_w = self_sum.total, cross_sum.total
    small = cross_w[:, 3 * width : 3 * width + 7].T
    return (
        combined[None],
        feature_grad[None],
        cross_w[None, :, :width],
        cross_w[None, :, width : 3 * width],
        self_w[None, :, 4 * width :],
        self_w[None, :, width : 4 * width],
        self_w[None, :, :width],
        in_w[None],
        out_w[None],
        gate_w[None],
        small[None, 0:6:2],
        small[None, 1:6:2],
        small[None, 6],
    )


def solution(mesh):
    rows = P("stream", "docs", None)
    weight = P("stream", None, None)
    return jax.shard_map(
        body,
        mesh=mesh,
        in_specs=(rows, rows, P("docs", None), P("docs", None)) + (weight,) * 10
        + (P("stream", None),),
        out_specs=(rows,) * 10 + (P("stream", None, "docs"),) * 2 + (P("stream", "docs"),),
        check_vma=False,
    )
```

```python
import functools

import jax
import jax.numpy as jnp
from jax import lax
from jax.experimental import pallas as pl
from jax.experimental.pallas import tpu as pltpu
from jax.sharding import PartitionSpec as P

HD = 64
PAIR = 2 * HD
SLOT = 96
FF_BLOCK = 512
VMEM_LIMIT = 60 << 20
F32 = jnp.float32
BF16 = jnp.bfloat16
norm_epsilon = 1e-06
masked_value = -1e30

VM = pltpu.VMEM
SM = pltpu.SMEM
HBM = pltpu.HBM
LAZY = "lazy"
PLACE = "place"


def nn(left, right):
    return lax.dot_general(left, right, (((1,), (0,)), ((), ())), preferred_element_type=F32)


def nt(left, right):
    return lax.dot_general(left, right, (((1,), (1,)), ((), ())), preferred_element_type=F32)


def padded_bytes(shape, dtype):
    size = jnp.dtype(dtype).itemsize
    shape = (1,) * (2 - len(shape)) + tuple(shape)
    tile = 32 // size
    total = -(-shape[-1] // 128) * 128 * -(-shape[-2] // tile) * tile * size
    for extent in shape[:-2]:
        total *= extent
    return total


class Arriving:
    def __init__(self, source, target, sem):
        self.copy, self.ref = fetch(source, target, sem), target

    def wait(self):
        if self.copy is not None:
            self.copy.wait()
            self.copy = None
        return self.ref


class Place:
    def __init__(self, text=None, visual=None):
        self.text, self.visual = text, visual

    def __getitem__(self, what):
        if what == 0:
            return lax.axis_index("stream")
        if what == 1:
            return lax.axis_index("docs") & 1
        if what == 5:
            return lax.axis_index("docs")
        return self.text[0, 0] if what == 2 else self.visual[0, what - 3]


def run_kernel(kernel, name, ins, outs, scratch=(), us=5.0, spare=6 << 20):
    counts = ()
    place = ins[0][1] is PLACE
    if place:
        counts, ins = ins[0][0], ins[1:]
    lazy = [at for at, (_, space) in enumerate(ins) if space is LAZY]
    scratch = list(scratch)
    own = len(scratch)
    scratch += [VM(ins[at][0].shape, ins[at][0].dtype) for at in lazy]
    if lazy:
        scratch.append(pltpu.SemaphoreType.DMA((len(lazy),)))
    need = sum(padded_bytes(array.shape, array.dtype) for array, space in ins if space is VM)
    need += sum(padded_bytes(shape, dtype) for shape, dtype, space in outs if space is VM)
    need += sum(
        padded_bytes(ref.shape, ref.dtype) for ref in scratch if hasattr(ref, "memory_space")
        and ref.memory_space == VM
    )

    def wrapped(*refs):
        front = (Place(*refs[: len(counts)]),) if place else ()
        refs = refs[len(counts) :]
        first = len(ins) + len(outs)
        operands = list(refs[: len(ins)])
        extra = refs[first + own :]
        for slot, at in enumerate(lazy):
            operands[at] = Arriving(operands[at], extra[slot], extra[-1].at[slot])
        kernel(*front, *operands, *refs[len(ins) : first + own])

    return pl.pallas_call(
        wrapped,
        name=name,
        in_specs=[pl.BlockSpec(memory_space=SM)] * len(counts)
        + [pl.BlockSpec(memory_space=HBM if space is LAZY else space) for _, space in ins],
        out_specs=[pl.BlockSpec(memory_space=space) for _, _, space in outs],
        out_shape=[jax.ShapeDtypeStruct(shape, dtype) for shape, dtype, _ in outs],
        scratch_shapes=scratch,
        compiler_params=pltpu.CompilerParams(vmem_limit_bytes=min(VMEM_LIMIT, need + spare)),
        cost_estimate=pl.CostEstimate(
            flops=int(us * 30e9), bytes_accessed=1000, transcendentals=0
        ),
    )(*counts, *[array for array, _ in ins])


def fetch(source, target, sem):
    copy = pltpu.make_async_copy(source, target, sem)
    copy.start()
    return copy


def normalise(resid):
    center = resid - jnp.mean(resid, axis=-1, keepdims=True)
    scale = lax.rsqrt(jnp.mean(center * center, axis=-1, keepdims=True) + norm_epsilon)
    return center * scale, scale


def normalise_back(grad, unit, scale, gain):
    gain_sum = jnp.sum(grad * unit, axis=0, keepdims=True)
    shift_sum = jnp.sum(grad, axis=0, keepdims=True)
    scaled = grad * gain
    first = jnp.mean(scaled, axis=-1, keepdims=True)
    second = jnp.mean(scaled * unit, axis=-1, keepdims=True)
    return scale * (scaled - first - unit * second), gain_sum, shift_sum


def attend(q_ref, q_at, k_ref, k_at, v_ref, v_at, bias_ref, out_ref, probs_ref):
    heads = out_ref.shape[1] // HD
    first = lax.broadcasted_iota(jnp.int32, (k_ref.shape[0], PAIR), 1) < HD
    queries, values, scores, probs, mixed = {}, {}, {}, {}, {}
    for turn in range(heads + 2):
        if turn < heads:
            pair, head = divmod(turn, 2)
            at = pair * PAIR
            if head == 0:
                queries[pair] = q_ref[:, q_at + at : q_at + at + PAIR] * jnp.asarray(
                    HD**-0.5, BF16
                )
            keys = k_ref[:, k_at + at : k_at + at + PAIR]
            zero = jnp.zeros_like(keys)
            own = jnp.where(first, keys, zero) if head == 0 else jnp.where(first, zero, keys)
            scores[turn] = nt(own, queries[pair])
        if 0 <= turn - 1 < heads:
            at = turn - 1
            raw = scores.pop(at) + bias_ref[...]
            shifted = jnp.exp(raw - jnp.max(raw, axis=0, keepdims=True))
            probs[at] = (shifted * (1.0 / jnp.sum(shifted, axis=0, keepdims=True))).astype(BF16)
            probs_ref[at] = probs[at]
        if 0 <= turn - 2:
            pair, head = divmod(turn - 2, 2)
            at = pair * PAIR
            if head == 0:
                values[pair] = v_ref[:, v_at + at : v_at + at + PAIR].T
            mixed[head] = nn(values[pair][head * HD : (head + 1) * HD], probs.pop(turn - 2))
            if head == 1:
                out_ref[:, at : at + PAIR] = (
                    jnp.concatenate([mixed[0], mixed[1]], axis=0).astype(BF16).T
                )


def attend_back(
    q_ref, q_at, k_ref, k_at, v_ref, v_at, mixed_ref, grad_ref, probs_ref,
    dq_ref, dq_at, dk_ref, dk_at, dv_ref, dv_at,
):
    heads = grad_ref.shape[1] // HD
    scale = HD**-0.5
    first = lax.broadcasted_iota(jnp.int32, (k_ref.shape[0], PAIR), 1) < HD

    def columns(ref, start, pair):
        return ref[:, start + pair * PAIR : start + (pair + 1) * PAIR]

    grads_t, inner, prob_grads, score_grads = {}, {}, {}, {}
    key_grads, value_grads, query_grads = {}, {}, {}
    for turn in range(heads + 2):
        if turn < heads:
            pair, head = divmod(turn, 2)
            if head == 0:
                grads_t[pair] = columns(grad_ref, 0, pair).T
                inner[pair] = grads_t[pair].astype(F32) * columns(mixed_ref, 0, pair).T.astype(F32)
            values = columns(v_ref, v_at, pair)
            zero = jnp.zeros_like(values)
            own = jnp.where(first, values, zero) if head == 0 else jnp.where(first, zero, values)
            prob_grads[turn] = nn(own, grads_t[pair])
        if 0 <= turn - 1 < heads:
            pair, head = divmod(turn - 1, 2)
            weighed = jnp.sum(inner[pair][head * HD : (head + 1) * HD], axis=0, keepdims=True)
            score_grads[turn - 1] = (
                probs_ref[turn - 1].astype(F32) * (prob_grads.pop(turn - 1) - weighed)
            ).astype(BF16)
        if 0 <= turn - 2:
            pair, head = divmod(turn - 2, 2)
            score_grad = score_grads.pop(turn - 2)
            key_grads[head] = nn(score_grad, columns(q_ref, q_at, pair))
            value_grads[head] = nn(probs_ref[turn - 2], columns(grad_ref, 0, pair))
            keys_t = columns(k_ref, k_at, pair).T
            query_grads[head] = nn(keys_t[head * HD : (head + 1) * HD], score_grad)
            if head == 1:
                at = pair * PAIR
                dk_ref[:, dk_at + at : dk_at + at + PAIR] = (
                    jnp.where(first, key_grads[0], key_grads[1]) * scale
                ).astype(BF16)
                dv_ref[:, dv_at + at : dv_at + at + PAIR] = jnp.where(
                    first, value_grads[0], value_grads[1]
                ).astype(BF16)
                dq_ref[:, dq_at + at : dq_at + at + PAIR] = (
                    (jnp.concatenate([query_grads[0], query_grads[1]], axis=0) * scale)
                    .astype(BF16)
                    .T
                )


def iota(shape, dim):
    return lax.broadcasted_iota(jnp.int32, shape, dim)


def text_doc(where, shape, dim):
    return (iota(shape, dim) >= where[2]).astype(jnp.int32)


def slot_doc(shape, dim):
    row = iota(shape, dim)
    return (row >= SLOT).astype(jnp.int32) + (row >= 2 * SLOT).astype(jnp.int32)


def slot_seen(where, shape, dim):
    row = iota(shape, dim)
    doc = slot_doc(shape, dim)
    count = jnp.where(doc == 0, where[3], jnp.where(doc == 1, where[4], 0))
    return row - doc * SLOT < count


def slot_key(where, shape, dim):
    return jnp.where(slot_seen(where, shape, dim), slot_doc(shape, dim), -1)


def picked(where, shape, packed_dim):
    doc = slot_doc(shape, packed_dim)
    place = iota(shape, packed_dim) - doc * SLOT + doc * where[2]
    same = (place == iota(shape, 1 - packed_dim)) & slot_seen(where, shape, packed_dim)
    return jnp.where(same, 1.0, 0.0).astype(BF16)


def set_bias(bias_ref, key_doc, query_doc):
    bias_ref[...] = jnp.where(key_doc == query_doc, 0.0, masked_value)


def own_valid(where, rows):
    seen = slot_seen(where, (rows, 1), 0)
    return jnp.where(seen | (where[0] == 0), 1.0, 0.0).astype(F32)


def put_split(split, core, value, at, sent_ref, kept_ref):
    cols = slice(at, at + value.shape[1])
    if not split:
        kept_ref[:, cols] = value.astype(BF16)
        return
    groups, piece = kept_ref.shape[:2]
    pieces = value.reshape(groups, 2, piece, value.shape[1]).astype(BF16)
    even = core == 0
    kept_ref[:, :, cols] = jnp.where(even, pieces[:, 0], pieces[:, 1])
    sent_ref[:, :, cols] = jnp.where(even, pieces[:, 1], pieces[:, 0])


def query_kernel(where, feat, wq, x_out, q_out, q_sent, pick, pick_t):
    packed = pick.shape[0]
    pick[...] = picked(where, pick.shape, 0)
    pick_t[...] = picked(where, pick_t.shape, 1)
    rows = feat.wait()

    @pl.when(where[0] == 0)
    def _():
        x_out[...] = rows[...]

    @pl.when(where[0] != 0)
    def _():
        x_out[:packed] = nn(pick[...], rows[...]).astype(BF16)
        x_out[packed:] = jnp.zeros((x_out.shape[0] - packed, x_out.shape[1]), BF16)

    q_out[...] = nn(x_out[...], wq.wait()[...]).astype(BF16)
    q_sent[...] = q_out[:packed]


def key_value_kernel(x, w, kv_out, kv_sent):
    kv_out[...] = nn(x[...], w[...]).astype(BF16)
    kv_sent[...] = kv_out[: kv_sent.shape[0]]


def vision_attend_kernel(where, q, kv, mixed, probs, bias):
    width = q.shape[1]

    @pl.when(where[0] == 0)
    def _():
        keys, queries = bias.shape
        set_bias(bias, text_doc(where, (keys, 1), 0), slot_doc((1, queries), 1))
        attend(q, 0, kv, 0, kv, width, bias, mixed, probs)


def own_attend_kernel(where, q, kv, mixed, probs, bias):
    width = q.shape[1]

    @pl.when(where[0] == 0)
    def _():
        keys, queries = bias.shape
        set_bias(bias, slot_key(where, (keys, 1), 0), text_doc(where, (1, queries), 1))
        attend(q, 0, kv, 0, kv, width, bias, mixed, probs)


def middle_kernel(
    where, x, own_mixed, vision_mixed, pick, gains, shifts, wo, wqkv, ws, wi, wf,
    mixed_hbm, first_low_hbm, unit1_hbm, scale1_hbm, qkv_hbm, self_low_hbm, self_probs_hbm,
    second_low_hbm, unit2_hbm, scale2_hbm, hidden_hbm, slope_hbm, unit3_hbm, scale3_hbm,
    third, third_low, third_sent,
    mixed, first_low, unit1, scale1, qkv, self_low, self_probs, second_low, unit2, scale2, hidden,
    slope, unit3, scale3, first, self_bias, save_sem,
):
    width = x.shape[1]
    rows = x.shape[0]
    packed = vision_mixed.shape[0]
    saves = []

    def save(source, target):
        saves.append(fetch(source, target, save_sem.at[len(saves)]))

    gain = gains[...].astype(F32)
    shift = shifts[...].astype(F32)

    @pl.when(where[0] == 0)
    def _():
        mixed[...] = own_mixed[...]
        set_bias(self_bias, text_doc(where, (rows, 1), 0), text_doc(where, (1, rows), 1))

    @pl.when(where[0] != 0)
    def _():
        mixed[:packed] = vision_mixed[...]
        mixed[packed:] = jnp.zeros((rows - packed, width), BF16)
        set_bias(self_bias, slot_key(where, (rows, 1), 0), slot_doc((1, rows), 1))

    save(mixed, mixed_hbm)
    unit, scale = normalise(x[...].astype(F32) + nn(mixed[...], wo.wait()[...]))
    unit1[...] = unit.astype(BF16)
    scale1[...] = jnp.broadcast_to(scale, scale1.shape)
    first[...] = unit * gain[0:1] + shift[0:1]
    first_low[...] = first[...].astype(BF16)
    save(unit1, unit1_hbm)
    save(scale1, scale1_hbm)
    save(first_low, first_low_hbm)
    qkv[...] = nn(first_low[...], wqkv.wait()[...]).astype(BF16)
    save(qkv, qkv_hbm)
    attend(qkv, 0, qkv, width, qkv, 2 * width, self_bias, self_low, self_probs)
    save(self_low, self_low_hbm)
    save(self_probs, self_probs_hbm)
    unit, scale = normalise(first[...] + nn(self_low[...], ws.wait()[...]))
    unit2[...] = unit.astype(BF16)
    scale2[...] = jnp.broadcast_to(scale, scale2.shape)
    third[...] = unit * gain[1:2] + shift[1:2]
    second_low[...] = third[...].astype(BF16)
    save(unit2, unit2_hbm)
    save(scale2, scale2_hbm)
    save(second_low, second_low_hbm)
    wi = wi.wait()
    wf = wf.wait()
    blocks = hidden.shape[1] // FF_BLOCK
    raw, active = {}, {}
    for turn in range(blocks + 2):
        if turn < blocks:
            raw[turn] = nn(second_low[...], wi[:, turn * FF_BLOCK : (turn + 1) * FF_BLOCK])
        if 0 <= turn - 1 < blocks:
            at = (turn - 1) * FF_BLOCK
            pre = raw.pop(turn - 1)
            below = 0.5 * (1.0 + lax.erf(pre * (2.0**-0.5)))
            density = jnp.exp(pre * pre * -0.5) * 0.3989422804014327
            active[turn - 1] = (pre * below).astype(BF16)
            hidden[:, at : at + FF_BLOCK] = active[turn - 1]
            slope[:, at : at + FF_BLOCK] = (below + pre * density).astype(BF16)
        if 0 <= turn - 2:
            at = (turn - 2) * FF_BLOCK
            third[...] += nn(active.pop(turn - 2), wf[at : at + FF_BLOCK, :])
    save(hidden, hidden_hbm)
    save(slope, slope_hbm)
    unit, scale = normalise(third[...])
    unit3[...] = unit.astype(BF16)
    scale3[...] = jnp.broadcast_to(scale, scale3.shape)
    save(unit3, unit3_hbm)
    save(scale3, scale3_hbm)
    third[...] = (unit * gain[2:3] + shift[2:3]) * own_valid(where, rows)
    third_low[...] = third[...].astype(BF16)

    @pl.when(where[0] == 0)
    def _():
        third_sent[...] = nn(pick[...], third_low[...]).astype(BF16)

    @pl.when(where[0] != 0)
    def _():
        third_sent[...] = third_low[:packed]

    for copy in saves:
        copy.wait()


def gate_own_kernel(where, third_low, pick, cot, bias, wg, logits, cot_rows):
    width = third_low.shape[1]
    packed = pick.shape[0]
    logits[...] = nn(third_low[...], wg[:width]) + bias[...].astype(F32)
    given = cot.wait()

    @pl.when(where[0] == 0)
    def _():
        cot_rows[...] = given[...]

    @pl.when(where[0] != 0)
    def _():
        cot_rows[:packed] = nn(pick[...], given[...]).astype(BF16)
        cot_rows[packed:] = jnp.zeros((cot_rows.shape[0] - packed, width), BF16)


def gate_kernel(
    where, third, other, own_logits, cot_rows, pick, pick_t, wg,
    combined, other_low, logit_low, own_part, sent, bias_sum,
):
    rows, width = third.shape
    packed = pick.shape[0]

    @pl.when(where[0] == 0)
    def _():
        other_low[...] = nn(pick_t[...], other[...]).astype(BF16)

    @pl.when(where[0] != 0)
    def _():
        other_low[:packed] = other[...]
        other_low[packed:] = jnp.zeros((rows - packed, width), BF16)

    valid = own_valid(where, rows)
    gate = jax.nn.sigmoid(own_logits[...] + nn(other_low[...], wg[width:]))
    other_rows = other_low[...].astype(F32)
    out_grad = cot_rows[...].astype(F32) * valid
    logit_grad = out_grad * (third[...] - other_rows) * gate * (1.0 - gate)
    bias_sum[...] = jnp.sum(logit_grad, axis=0, keepdims=True)
    logit_low[...] = logit_grad.astype(BF16)
    own_part[...] = nt(logit_low[...], wg[:width]) + out_grad * gate
    partner = (nt(logit_low[...], wg[width:]) + out_grad * (1.0 - gate)).astype(BF16)
    mixed = valid * (gate * third[...] + (1.0 - gate) * other_rows)

    @pl.when(where[0] == 0)
    def _():
        combined[...] = mixed
        sent[...] = nn(pick[...], partner).astype(BF16)

    @pl.when(where[0] != 0)
    def _():
        high = mixed[:packed].astype(BF16)
        rest = (mixed[:packed] - high.astype(F32)).astype(BF16)
        combined[...] = nn(pick_t[...], high) + nn(pick_t[...], rest)
        sent[...] = partner[:packed]


def gate_weight_kernel(split, where, own, other, grad, *outs):
    sent, kept = outs if split else (None,) + outs
    half = own.shape[1]
    full = kept.shape[0] * kept.shape[1] * 2 if split else kept.shape[0]
    for part, left in enumerate((own, other)):
        value = nn(left[...].T, grad[...])
        if split:
            rows = kept.shape[0] * half // full
            put_split(
                split, where[1], value, 0,
                sent.at[pl.ds(part * rows, rows)], kept.at[pl.ds(part * rows, rows)],
            )
        else:
            kept[pl.ds(part * half, half)] = value.astype(BF16)


def third_back_kernel(
    split, where, own_part, returned, pick_t, unit, scale, gains, hidden,
    grad_out, low_out, sums, *rest,
):
    grad = rest[-1]
    kept = rest[-2]
    rows = own_part.shape[0]
    packed = returned.shape[0]
    grad[...] = own_part[...]

    @pl.when(where[0] == 0)
    def _():
        grad[...] += nn(pick_t[...], returned[...])

    @pl.when(where[0] != 0)
    def _():
        grad[:packed] += returned[...].astype(F32)

    value, gain_sum, shift_sum = normalise_back(
        grad[...] * own_valid(where, rows),
        unit.wait()[...].astype(F32),
        scale.wait()[:, 0:1],
        gains[2:3].astype(F32),
    )
    grad_out[...] = value
    low_out[...] = value.astype(BF16)
    sums[0:1] = gain_sum
    sums[1:2] = shift_sum
    hidden = hidden.wait()
    if split:
        sent = rest[0]
        groups, piece = kept.shape[:2]
        even = where[1] == 0
        for group in range(groups):
            left = hidden[:, group * 2 * piece : (group + 1) * 2 * piece].T
            value = nn(left, low_out[...]).astype(BF16)
            kept[group] = jnp.where(even, value[:piece], value[piece:])
            sent[group] = jnp.where(even, value[piece:], value[:piece])
    else:
        for at in range(0, hidden.shape[1], FF_BLOCK):
            left = hidden[:, at : at + FF_BLOCK].T
            kept[at : at + FF_BLOCK] = nn(left, low_out[...]).astype(BF16)


def ffn_back_kernel(
    split, where, third_grad, third_low, wf, slope, second_low, wi, total, *rest
):
    sent, kept, left = rest if split else (None,) + rest
    wf = wf.wait()
    slope = slope.wait()
    total[...] = third_grad[...]
    left[...] = second_low.wait()[...].T
    wi = wi.wait()
    blocks = wi.shape[1] // FF_BLOCK
    back, pre_low = {}, {}
    for turn in range(blocks + 2):
        if turn < blocks:
            back[turn] = nt(third_low[...], wf[turn * FF_BLOCK : (turn + 1) * FF_BLOCK, :])
        if 0 <= turn - 1 < blocks:
            at = (turn - 1) * FF_BLOCK
            pre_low[turn - 1] = (
                back.pop(turn - 1) * slope[:, at : at + FF_BLOCK].astype(F32)
            ).astype(BF16)
        if 0 <= turn - 2:
            at = (turn - 2) * FF_BLOCK
            value = pre_low.pop(turn - 2)
            total[...] += nt(value, wi[:, at : at + FF_BLOCK])
            put_split(split, where[1], nn(left[...], value), at, sent, kept)


def second_back_kernel(total, unit, scale, gains, ws, grad_out, low_out, mixed_grad, sums):
    value, gain_sum, shift_sum = normalise_back(
        total[...], unit.wait()[...].astype(F32), scale.wait()[:, 0:1], gains[1:2].astype(F32)
    )
    grad_out[...] = value
    low_out[...] = value.astype(BF16)
    sums[0:1] = gain_sum
    sums[1:2] = shift_sum
    mixed_grad[...] = nt(low_out[...], ws.wait()[...]).astype(BF16)


def self_back_kernel(
    second_grad, mixed_grad, gains, qkv, self_low, probs, wqkv, unit, scale, wo,
    dqkv, grad_out, low_out, cross, cross_sent, sums,
):
    width = second_grad.shape[1]
    qkv = qkv.wait()
    attend_back(
        qkv, 0, qkv, width, qkv, 2 * width, self_low.wait(), mixed_grad, probs.wait(),
        dqkv, 0, dqkv, width, dqkv, 2 * width,
    )
    value, gain_sum, shift_sum = normalise_back(
        second_grad[...] + nt(dqkv[...], wqkv.wait()[...]),
        unit.wait()[...].astype(F32),
        scale.wait()[:, 0:1],
        gains[0:1].astype(F32),
    )
    grad_out[...] = value
    low_out[...] = value.astype(BF16)
    sums[0:1] = gain_sum
    sums[1:2] = shift_sum
    cross[...] = nt(low_out[...], wo.wait()[...]).astype(BF16)
    cross_sent[...] = cross[: cross_sent.shape[0]]


def self_weight_kernel(
    split, where, dqkv, second_grad, first_grad, first_sums, second_sums, third_sums, bias_sum,
    first_low, self_low, mixed, *outs,
):
    sent, kept, more_sent, more_kept = outs if split else (None, outs[0], None, outs[1])
    width = second_grad.shape[1]
    left = first_low.wait()[...].T
    for part in range(3):
        value = nn(left, dqkv[:, part * width : (part + 1) * width])
        put_split(split, where[1], value, part * width, sent, kept)
    value = nn(self_low.wait()[...].T, second_grad[...])
    put_split(split, where[1], value, 0, more_sent, more_kept)
    value = nn(mixed.wait()[...].T, first_grad[...])
    put_split(split, where[1], value, width, more_sent, more_kept)
    small = jnp.concatenate(
        [first_sums[...], second_sums[...], third_sums[...], bias_sum[...],
         jnp.zeros((121, width), F32)], axis=0,
    )
    put_split(split, where[1], small.T, 2 * width, more_sent, more_kept)


def vision_back_kernel(where, q, kv, mixed, grad, probs, own, sent):
    width = q.shape[1]
    kv, probs = kv.wait(), probs.wait()

    @pl.when(where[0] == 0)
    def _():
        attend_back(q, 0, kv, 0, kv, width, mixed, grad, probs, sent, 0, own, 0, own, width)


def cross_back_kernel(where, q, kv, mixed, grad, probs, own, sent):
    width = kv.shape[1] // 2
    q, mixed, probs = q.wait(), mixed.wait(), probs.wait()

    @pl.when(where[0] == 0)
    def _():
        attend_back(q, 0, kv, 0, kv, width, mixed, grad, probs, own, 0, sent, 0, sent, width)


def cross_weight_kernel(
    split, place, own_query, own_key_value, query, key_value, x, dqkv, left, *outs
):
    sent, kept = outs if split else (None,) + outs
    width = own_query.shape[1]
    packed = query.shape[0]

    @pl.when(place[0] == 0)
    def _():
        dqkv[:, :width] = own_query[...]
        dqkv[:, width:] = own_key_value[...]

    @pl.when(place[0] != 0)
    def _():
        dqkv[:packed, :width] = query[...]
        dqkv[:packed, width:] = key_value[...]
        dqkv[packed:] = jnp.zeros((dqkv.shape[0] - packed, dqkv.shape[1]), BF16)

    left[...] = x.wait()[...].T
    for part in range(2):
        value = nn(left[...], dqkv[:, (1 + part) * width : (2 + part) * width])
        put_split(split, place[1], value, part * width, sent, kept)


def query_weight_kernel(split, place, left, dqkv, *outs):
    sent, kept = outs if split else (None,) + outs
    put_split(split, place[1], nn(left[...], dqkv[:, : left.shape[0]]), 0, sent, kept)


def feature_kernel(where, dqkv, first_grad, pick_t, wq, wkv, out, total):
    width = first_grad.shape[1]
    packed = pick_t.shape[1]
    total[...] = first_grad[...] + nt(dqkv[:, :width], wq.wait()[...])
    total[...] += nt(dqkv[:, width:], wkv.wait()[...])

    @pl.when(where[0] == 0)
    def _():
        out[...] = total[...]

    @pl.when(where[0] != 0)
    def _():
        value = total[:packed]
        high = value.astype(BF16)
        rest = (value - high.astype(F32)).astype(BF16)
        out[...] = nn(pick_t[...], high) + nn(pick_t[...], rest)


def to_partner(shard):
    return lax.ppermute(shard, "stream", [(0, 1), (1, 0)])


def to_language(shard):
    return lax.ppermute(shard, "stream", [(1, 0)])


def to_vision(shard):
    return lax.ppermute(shard, "stream", [(0, 1)])


def swap(shard, bit):
    count = lax.axis_size("docs")
    return lax.ppermute(shard, "docs", [(i, i ^ 1 << bit) for i in range(count)])


def after(value, *others):
    return lax.optimization_barrier((value,) + others)[0] if others else value


def combine_kernel(bit, where, kept, arrived, sent, rest):
    mine = (where[5] >> bit) & 1
    sent[...] = kept[:, 1 - mine] + arrived[:, 1 - mine]
    rest[...] = kept[:, mine] + arrived[:, mine]


def finish_kernel(parts, kept, arrived, *outs):
    for (start, stop), out in zip(parts, outs):
        out[...] = kept[:, start:stop].astype(F32) + arrived[:, start:stop].astype(F32)


class Summation:
    def __init__(self, parts, first=0):
        index = lax.axis_index("docs")
        count = lax.axis_size("docs")
        self.names = list(range(count.bit_length() - 2, 0, -1))
        bits = list(range(1, count.bit_length() - 1))
        self.order = bits if first == 0 else bits[1:] + bits[:1]
        if len(parts) == 2:
            sent, kept = parts
        else:
            full = parts[0].reshape(count // 2, 2, -1, parts[0].shape[-1])
            core = index & 1
            sent = lax.dynamic_index_in_dim(full, 1 - core, 1, keepdims=False)
            kept = lax.dynamic_index_in_dim(full, core, 1, keepdims=False)
        self.kept = kept
        self.arrived = swap(sent, 0)

    def advance(self, *earlier):
        bit = self.order.pop(0)
        axis = self.names.index(bit)
        ahead, behind = 2**axis, 2 ** (len(self.names) - 1 - axis)
        self.names.pop(axis)
        tail = self.kept.shape[-2:]
        shape = (ahead, 2, behind) + tail
        half = ((ahead, behind) + tail, BF16, VM)
        self.sent, kept = run_kernel(
            functools.partial(combine_kernel, bit), "combine",
            [((), PLACE), (self.kept.reshape(shape), VM),
             (after(self.arrived, *earlier).reshape(shape), VM)],
            [half, half], us=1.0,
        )
        self.kept = kept
        self.arrived = swap(self.sent, bit)

    def finish(self, parts, *earlier):
        while self.order:
            self.advance(*earlier)
        shape = self.kept.shape[-2:]
        return run_kernel(
            functools.partial(finish_kernel, parts), "finish",
            [(self.kept.reshape(shape), VM), (after(self.arrived, *earlier).reshape(shape), VM)],
            [((shape[0], stop - start), F32, VM) for start, stop in parts], us=1.0,
        )


def body(
    block_features, cotangent, text_counts, visual_counts, w_cross_q, w_cross_kv, w_cross_out,
    w_self_qkv, w_self_out, w_ffn_in, w_ffn_out, w_gate, ln_gain, ln_bias, gate_bias,
):
    feat = block_features[0]
    rows, width = feat.shape
    wq, wkv, wo = w_cross_q[0], w_cross_kv[0], w_cross_out[0]
    wqkv, ws = w_self_qkv[0], w_self_out[0]
    wi, wf, wg = w_ffn_in[0], w_ffn_out[0], w_gate[0]
    gains, shifts = ln_gain[0], ln_bias[0]
    hidden_width = wi.shape[1]
    count = lax.axis_size("docs")
    groups = count // 2
    split = (width // count) % 16 == 0
    packed = text_counts.shape[1] * SLOT
    heads = width // HD
    where = (text_counts, visual_counts)
    here = ()
    dma = pltpu.SemaphoreType.DMA
    low = ((rows, width), BF16, VM)
    wide = ((rows, width), F32, VM)
    sums = ((2, width), F32, VM)
    few = ((packed, width), BF16, VM)

    def weight_outs(total_rows, columns):
        if split:
            shape = (groups, total_rows // count, columns)
            return [(shape, BF16, VM), (shape, BF16, VM)]
        return [((total_rows, columns), BF16, VM)]

    parts = 2 if split else 1
    x, q, q_sent, pick, pick_t = run_kernel(
        query_kernel, "query",
        [(where, PLACE), (feat, LAZY), (wq, LAZY)],
        [low, low, few, ((packed, rows), BF16, VM), ((rows, packed), BF16, VM)],
    )
    vision_q = to_language(q_sent)
    kv, kv_sent = run_kernel(
        key_value_kernel, "key_value",
        [(after(x, q_sent), VM), (wkv, VM)],
        [((rows, 2 * width), BF16, VM), ((packed, 2 * width), BF16, VM)],
    )
    vision_kv = to_language(kv_sent)
    vision_mixed, vision_probs = run_kernel(
        vision_attend_kernel, "vision_attend",
        [(where, PLACE), (vision_q, VM), (after(kv, kv_sent), VM)],
        [few, ((heads, rows, packed), BF16, VM)],
        [VM((rows, packed), F32)],
    )
    vision_mixed_here = to_vision(vision_mixed)
    own_mixed, cross_probs = run_kernel(
        own_attend_kernel, "own_attend",
        [(where, PLACE), (q, VM), (after(vision_kv, vision_mixed), VM)],
        [low, ((heads, packed, rows), BF16, VM)],
        [VM((packed, rows), F32)],
    )

    def state(*shape, kind=BF16):
        return (shape, kind, HBM)

    full = state(rows, width)
    lane = state(rows, 128, kind=F32)
    saved = [
        full, full, full, lane, state(rows, 3 * width), full, state(heads, rows, rows), full, full,
        lane, state(rows, hidden_width), state(rows, hidden_width), full, lane,
    ]
    (
        mixed, first_low, unit1, scale1, qkv, self_low, self_probs, second_low, unit2, scale2,
        hidden, slope, unit3, scale3, third, third_low, third_sent,
    ) = run_kernel(
        middle_kernel, "middle",
        [(where, PLACE), (x, VM), (own_mixed, VM), (after(vision_mixed_here, own_mixed), VM),
         (pick, VM), (gains, VM), (shifts, VM)] + [(w, LAZY) for w in (wo, wqkv, ws, wi, wf)],
        saved + [wide, low, few],
        [VM(shape, kind) for shape, kind, _ in saved]
        + [VM((rows, width), F32), VM((rows, rows), F32), dma((len(saved),))],
    )
    other = to_partner(third_sent)
    own_logits, cot_rows = run_kernel(
        gate_own_kernel, "gate_own",
        [(here, PLACE), (after(third_low, third_sent), VM), (pick, VM), (cotangent[0], LAZY),
         (gate_bias, VM), (wg, VM)],
        [wide, low],
    )
    combined, other_low, logit_low, own_part, partner_sent, bias_sum = run_kernel(
        gate_kernel, "gate",
        [(where, PLACE), (third, VM), (after(other, own_logits), VM), (own_logits, VM),
         (cot_rows, VM), (pick, VM), (pick_t, VM), (wg, VM)],
        [wide, low, low, wide, few, ((1, width), F32, VM)],
    )
    returned = to_partner(partner_sent)
    gate_parts = run_kernel(
        functools.partial(gate_weight_kernel, split), "gate_weight",
        [(here, PLACE), (third_low, VM), (other_low, VM), (after(logit_low, partner_sent), VM)],
        weight_outs(2 * width, width),
    )
    gate_sum = Summation(gate_parts, 0)
    gate_sum.advance()
    third_back = run_kernel(
        functools.partial(third_back_kernel, split), "third_back",
        [(where, PLACE), (own_part, VM), (after(returned, gate_sum.sent), VM), (pick_t, VM),
         (unit3, LAZY), (scale3, LAZY), (gains, VM), (hidden, LAZY)],
        [wide, low, sums] + weight_outs(hidden_width, width),
        [VM((rows, width), F32)],
    )
    third_grad, third_grad_low, third_sums = third_back[:3]
    out_sum = Summation(third_back[3:], 1)
    ffn_back = run_kernel(
        functools.partial(ffn_back_kernel, split), "ffn_back",
        [(here, PLACE), (third_grad, VM), (after(third_grad_low, *third_back[3:]), VM), (wf, LAZY),
         (slope, LAZY), (second_low, LAZY), (wi, LAZY)],
        [wide] + weight_outs(width, hidden_width),
        [VM((width, rows), BF16)],
    )
    in_sum = Summation(ffn_back[1:], 0)
    out_sum.advance(ffn_back[0])
    second_grad, second_grad_low, mixed_grad, second_sums = run_kernel(
        second_back_kernel, "second_back",
        [(after(ffn_back[0], out_sum.sent, *ffn_back[1:]), VM), (unit2, LAZY), (scale2, LAZY),
         (gains, VM), (ws, LAZY)],
        [wide, low, low, sums],
    )
    in_sum.advance(second_sums)
    dqkv, first_grad, first_grad_low, cross_grad, cross_grad_sent, first_sums = run_kernel(
        self_back_kernel, "self_back",
        [(second_grad, VM), (after(mixed_grad, in_sum.sent), VM), (gains, VM),
         (qkv, LAZY), (self_low, LAZY), (self_probs, LAZY), (wqkv, LAZY), (unit1, LAZY),
         (scale1, LAZY), (wo, LAZY)],
        [((rows, 3 * width), BF16, VM), wide, low, low, few, sums],
    )
    vision_grad = to_language(cross_grad_sent)
    gate_sum.advance(first_sums)
    self_parts = run_kernel(
        functools.partial(self_weight_kernel, split), "self_weight",
        [(here, PLACE), (after(dqkv, cross_grad_sent, gate_sum.sent), VM), (second_grad_low, VM),
         (first_grad_low, VM), (first_sums, VM), (second_sums, VM), (third_sums, VM),
         (bias_sum, VM), (first_low, LAZY), (self_low, LAZY), (mixed, LAZY)],
        weight_outs(width, 3 * width) + weight_outs(width, 2 * width + 128),
    )
    self_sum = Summation(self_parts[:parts], 0)
    more_sum = Summation(self_parts[parts:], 0)
    gate_sum.advance(*self_parts)
    out_sum.advance(gate_sum.sent)
    own_key_value, query_sent = run_kernel(
        vision_back_kernel, "vision_back",
        [(here, PLACE), (vision_q, VM), (kv, LAZY), (vision_mixed, VM),
         (after(vision_grad, out_sum.sent, *self_parts), VM), (vision_probs, LAZY)],
        [((rows, 2 * width), BF16, VM), few],
    )
    query_here = to_vision(query_sent)
    self_sum.advance(query_sent)
    more_sum.advance(self_sum.sent)
    in_sum.advance(more_sum.sent)
    (gate_grad,) = gate_sum.finish([(0, width)], in_sum.sent)
    own_query, key_value_sent = run_kernel(
        cross_back_kernel, "cross_back",
        [(here, PLACE), (q, LAZY), (vision_kv, VM), (mixed, LAZY),
         (after(cross_grad, query_here, gate_grad), VM),
         (cross_probs, LAZY)],
        [low, ((packed, 2 * width), BF16, VM)],
    )
    key_value_here = to_vision(key_value_sent)
    out_sum.advance(key_value_sent)
    self_sum.advance(out_sum.sent)
    cross_out = run_kernel(
        functools.partial(cross_weight_kernel, split), "cross_weight",
        [(here, PLACE), (own_query, VM), (own_key_value, VM), (query_here, VM),
         (after(key_value_here, self_sum.sent), VM), (x, LAZY)],
        [((rows, 3 * width), BF16, VM), ((width, rows), BF16, VM)]
        + weight_outs(width, 2 * width),
    )
    dcross, left = cross_out[:2]
    cross_sum = Summation(cross_out[2:], 0)
    last_parts = run_kernel(
        functools.partial(query_weight_kernel, split), "query_weight",
        [(here, PLACE), (left, VM), (after(dcross, *cross_out[2:]), VM)],
        weight_outs(width, width),
    )
    last_sum = Summation(last_parts, 1)
    cross_sum.advance(*last_parts)
    in_sum.advance(cross_sum.sent)
    last_sum.advance(in_sum.sent)
    more_sum.advance(last_sum.sent)
    (feature_grad,) = run_kernel(
        feature_kernel, "feature",
        [(here, PLACE), (after(dcross, more_sum.sent), VM), (first_grad, VM), (pick_t, VM),
         (wq, LAZY), (wkv, LAZY)],
        [wide],
        [VM((rows, width), F32)],
    )
    self_sum.advance(feature_grad)
    (ffn_out_grad,) = out_sum.finish([(0, width)], self_sum.sent)
    (ffn_in_grad,) = in_sum.finish([(0, hidden_width)], ffn_out_grad)
    last_sum.advance(ffn_in_grad)
    more_sum.advance(last_sum.sent)
    cross_sum.advance(more_sum.sent)
    (self_qkv_grad,) = self_sum.finish([(0, 3 * width)], cross_sum.sent)
    last_sum.advance(self_qkv_grad)
    cross_sum.advance(last_sum.sent)
    self_out_grad, cross_out_grad, small = more_sum.finish(
        [(0, width), (width, 2 * width), (2 * width, 2 * width + 128)], cross_sum.sent
    )
    (cross_q_grad,) = last_sum.finish([(0, width)], self_out_grad)
    (cross_kv_grad,) = cross_sum.finish([(0, 2 * width)])
    small = small[:, :7].T
    return (
        combined[None],
        feature_grad[None],
        cross_q_grad[None],
        cross_kv_grad[None],
        cross_out_grad[None],
        self_qkv_grad[None],
        self_out_grad[None],
        ffn_in_grad[None],
        ffn_out_grad[None],
        gate_grad[None],
        small[None, 0:6:2],
        small[None, 1:6:2],
        small[None, 6],
    )


def solution(mesh):
    rows = P("stream", "docs", None)
    weight = P("stream", None, None)
    return jax.shard_map(
        body,
        mesh=mesh,
        in_specs=(rows, rows, P("docs", None), P("docs", None)) + (weight,) * 10
        + (P("stream", None),),
        out_specs=(rows,) * 10 + (P("stream", None, "docs"),) * 2 + (P("stream", "docs"),),
        check_vma=False,
    )
```

```python
import functools

import jax
import jax.numpy as jnp
from jax import lax
from jax.experimental import pallas as pl
from jax.experimental.pallas import tpu as pltpu
from jax.sharding import PartitionSpec as P

HD = 64
PAIR = 2 * HD
SLOT = 96
FF_BLOCK = 512
VMEM_LIMIT = 60 << 20
F32 = jnp.float32
BF16 = jnp.bfloat16
norm_epsilon = 1e-06
masked_value = -1e30

VM = pltpu.VMEM
SM = pltpu.SMEM
HBM = pltpu.HBM
LAZY = "lazy"
PLACE = "place"


def nn(left, right):
    return lax.dot_general(left, right, (((1,), (0,)), ((), ())), preferred_element_type=F32)


def nt(left, right):
    return lax.dot_general(left, right, (((1,), (1,)), ((), ())), preferred_element_type=F32)


def padded_bytes(shape, dtype):
    size = jnp.dtype(dtype).itemsize
    shape = (1,) * (2 - len(shape)) + tuple(shape)
    tile = 32 // size
    total = -(-shape[-1] // 128) * 128 * -(-shape[-2] // tile) * tile * size
    for extent in shape[:-2]:
        total *= extent
    return total


class Arriving:
    def __init__(self, source, target, sem):
        self.copy, self.ref = fetch(source, target, sem), target

    def wait(self):
        if self.copy is not None:
            self.copy.wait()
            self.copy = None
        return self.ref


class Place:
    def __init__(self, text=None, visual=None):
        self.text, self.visual = text, visual

    def __getitem__(self, what):
        if what == 0:
            return lax.axis_index("stream")
        if what == 1:
            return lax.axis_index("docs") & 1
        if what == 5:
            return lax.axis_index("docs")
        return self.text[0, 0] if what == 2 else self.visual[0, what - 3]


def run_kernel(kernel, name, ins, outs, scratch=(), us=5.0, spare=6 << 20):
    counts = ()
    place = ins[0][1] is PLACE
    if place:
        counts, ins = ins[0][0], ins[1:]
    lazy = [at for at, (_, space) in enumerate(ins) if space is LAZY]
    scratch = list(scratch)
    own = len(scratch)
    scratch += [VM(ins[at][0].shape, ins[at][0].dtype) for at in lazy]
    if lazy:
        scratch.append(pltpu.SemaphoreType.DMA((len(lazy),)))
    need = sum(padded_bytes(array.shape, array.dtype) for array, space in ins if space is VM)
    need += sum(padded_bytes(shape, dtype) for shape, dtype, space in outs if space is VM)
    need += sum(
        padded_bytes(ref.shape, ref.dtype) for ref in scratch if hasattr(ref, "memory_space")
        and ref.memory_space == VM
    )

    def wrapped(*refs):
        front = (Place(*refs[: len(counts)]),) if place else ()
        refs = refs[len(counts) :]
        first = len(ins) + len(outs)
        operands = list(refs[: len(ins)])
        extra = refs[first + own :]
        for slot, at in enumerate(lazy):
            operands[at] = Arriving(operands[at], extra[slot], extra[-1].at[slot])
        kernel(*front, *operands, *refs[len(ins) : first + own])

    return pl.pallas_call(
        wrapped,
        name=name,
        in_specs=[pl.BlockSpec(memory_space=SM)] * len(counts)
        + [pl.BlockSpec(memory_space=HBM if space is LAZY else space) for _, space in ins],
        out_specs=[pl.BlockSpec(memory_space=space) for _, _, space in outs],
        out_shape=[jax.ShapeDtypeStruct(shape, dtype) for shape, dtype, _ in outs],
        scratch_shapes=scratch,
        compiler_params=pltpu.CompilerParams(vmem_limit_bytes=min(VMEM_LIMIT, need + spare)),
        cost_estimate=pl.CostEstimate(
            flops=int(us * 30e9), bytes_accessed=1000, transcendentals=0
        ),
    )(*counts, *[array for array, _ in ins])


def fetch(source, target, sem):
    copy = pltpu.make_async_copy(source, target, sem)
    copy.start()
    return copy


def normalise(resid):
    center = resid - jnp.mean(resid, axis=-1, keepdims=True)
    scale = lax.rsqrt(jnp.mean(center * center, axis=-1, keepdims=True) + norm_epsilon)
    return center * scale, scale


def normalise_back(grad, unit, scale, gain):
    gain_sum = jnp.sum(grad * unit, axis=0, keepdims=True)
    shift_sum = jnp.sum(grad, axis=0, keepdims=True)
    scaled = grad * gain
    first = jnp.mean(scaled, axis=-1, keepdims=True)
    second = jnp.mean(scaled * unit, axis=-1, keepdims=True)
    return scale * (scaled - first - unit * second), gain_sum, shift_sum


def attend(q_ref, q_at, k_ref, k_at, v_ref, v_at, bias_ref, out_ref, probs_ref):
    heads = out_ref.shape[1] // HD
    first = lax.broadcasted_iota(jnp.int32, (k_ref.shape[0], PAIR), 1) < HD
    queries, values, scores, probs, mixed = {}, {}, {}, {}, {}
    for turn in range(heads + 2):
        if turn < heads:
            pair, head = divmod(turn, 2)
            at = pair * PAIR
            if head == 0:
                queries[pair] = q_ref[:, q_at + at : q_at + at + PAIR] * jnp.asarray(
                    HD**-0.5, BF16
                )
            keys = k_ref[:, k_at + at : k_at + at + PAIR]
            zero = jnp.zeros_like(keys)
            own = jnp.where(first, keys, zero) if head == 0 else jnp.where(first, zero, keys)
            scores[turn] = nt(own, queries[pair])
        if 0 <= turn - 1 < heads:
            at = turn - 1
            raw = scores.pop(at) + bias_ref[...]
            shifted = jnp.exp(raw - jnp.max(raw, axis=0, keepdims=True))
            probs[at] = (shifted * (1.0 / jnp.sum(shifted, axis=0, keepdims=True))).astype(BF16)
            probs_ref[at] = probs[at]
        if 0 <= turn - 2:
            pair, head = divmod(turn - 2, 2)
            at = pair * PAIR
            if head == 0:
                values[pair] = v_ref[:, v_at + at : v_at + at + PAIR].T
            mixed[head] = nn(values[pair][head * HD : (head + 1) * HD], probs.pop(turn - 2))
            if head == 1:
                out_ref[:, at : at + PAIR] = (
                    jnp.concatenate([mixed[0], mixed[1]], axis=0).astype(BF16).T
                )


def attend_back(
    q_ref, q_at, k_ref, k_at, v_ref, v_at, mixed_ref, grad_ref, probs_ref,
    dq_ref, dq_at, dk_ref, dk_at, dv_ref, dv_at,
):
    heads = grad_ref.shape[1] // HD
    scale = HD**-0.5
    first = lax.broadcasted_iota(jnp.int32, (k_ref.shape[0], PAIR), 1) < HD

    def columns(ref, start, pair):
        return ref[:, start + pair * PAIR : start + (pair + 1) * PAIR]

    grads_t, inner, prob_grads, score_grads = {}, {}, {}, {}
    key_grads, value_grads, query_grads = {}, {}, {}
    for turn in range(heads + 2):
        if turn < heads:
            pair, head = divmod(turn, 2)
            if head == 0:
                grads_t[pair] = columns(grad_ref, 0, pair).T
                inner[pair] = grads_t[pair].astype(F32) * columns(mixed_ref, 0, pair).T.astype(F32)
            values = columns(v_ref, v_at, pair)
            zero = jnp.zeros_like(values)
            own = jnp.where(first, values, zero) if head == 0 else jnp.where(first, zero, values)
            prob_grads[turn] = nn(own, grads_t[pair])
        if 0 <= turn - 1 < heads:
            pair, head = divmod(turn - 1, 2)
            weighed = jnp.sum(inner[pair][head * HD : (head + 1) * HD], axis=0, keepdims=True)
            score_grads[turn - 1] = (
                probs_ref[turn - 1].astype(F32) * (prob_grads.pop(turn - 1) - weighed)
            ).astype(BF16)
        if 0 <= turn - 2:
            pair, head = divmod(turn - 2, 2)
            score_grad = score_grads.pop(turn - 2)
            key_grads[head] = nn(score_grad, columns(q_ref, q_at, pair))
            value_grads[head] = nn(probs_ref[turn - 2], columns(grad_ref, 0, pair))
            keys_t = columns(k_ref, k_at, pair).T
            query_grads[head] = nn(keys_t[head * HD : (head + 1) * HD], score_grad)
            if head == 1:
                at = pair * PAIR
                dk_ref[:, dk_at + at : dk_at + at + PAIR] = (
                    jnp.where(first, key_grads[0], key_grads[1]) * scale
                ).astype(BF16)
                dv_ref[:, dv_at + at : dv_at + at + PAIR] = jnp.where(
                    first, value_grads[0], value_grads[1]
                ).astype(BF16)
                dq_ref[:, dq_at + at : dq_at + at + PAIR] = (
                    (jnp.concatenate([query_grads[0], query_grads[1]], axis=0) * scale)
                    .astype(BF16)
                    .T
                )


def iota(shape, dim):
    return lax.broadcasted_iota(jnp.int32, shape, dim)


def text_doc(where, shape, dim):
    return (iota(shape, dim) >= where[2]).astype(jnp.int32)


def slot_doc(shape, dim):
    row = iota(shape, dim)
    return (row >= SLOT).astype(jnp.int32) + (row >= 2 * SLOT).astype(jnp.int32)


def slot_seen(where, shape, dim):
    row = iota(shape, dim)
    doc = slot_doc(shape, dim)
    count = jnp.where(doc == 0, where[3], jnp.where(doc == 1, where[4], 0))
    return row - doc * SLOT < count


def slot_key(where, shape, dim):
    return jnp.where(slot_seen(where, shape, dim), slot_doc(shape, dim), -1)


def picked(where, shape, packed_dim):
    doc = slot_doc(shape, packed_dim)
    place = iota(shape, packed_dim) - doc * SLOT + doc * where[2]
    same = (place == iota(shape, 1 - packed_dim)) & slot_seen(where, shape, packed_dim)
    return jnp.where(same, 1.0, 0.0).astype(BF16)


def set_bias(bias_ref, key_doc, query_doc):
    bias_ref[...] = jnp.where(key_doc == query_doc, 0.0, masked_value)


def own_valid(where, rows):
    seen = slot_seen(where, (rows, 1), 0)
    return jnp.where(seen | (where[0] == 0), 1.0, 0.0).astype(F32)


def put_split(split, core, value, at, sent_ref, kept_ref):
    cols = slice(at, at + value.shape[1])
    if not split:
        kept_ref[:, cols] = value.astype(BF16)
        return
    groups, piece = kept_ref.shape[:2]
    pieces = value.reshape(groups, 2, piece, value.shape[1]).astype(BF16)
    even = core == 0
    kept_ref[:, :, cols] = jnp.where(even, pieces[:, 0], pieces[:, 1])
    sent_ref[:, :, cols] = jnp.where(even, pieces[:, 1], pieces[:, 0])


def query_kernel(where, feat, wq, x_out, q_out, q_sent, pick, pick_t):
    packed = pick.shape[0]
    pick[...] = picked(where, pick.shape, 0)
    pick_t[...] = picked(where, pick_t.shape, 1)
    rows = feat.wait()

    @pl.when(where[0] == 0)
    def _():
        x_out[...] = rows[...]

    @pl.when(where[0] != 0)
    def _():
        x_out[:packed] = nn(pick[...], rows[...]).astype(BF16)
        x_out[packed:] = jnp.zeros((x_out.shape[0] - packed, x_out.shape[1]), BF16)

    q_out[...] = nn(x_out[...], wq.wait()[...]).astype(BF16)
    q_sent[...] = q_out[:packed]


def key_value_kernel(x, w, kv_out, kv_sent):
    kv_out[...] = nn(x[...], w[...]).astype(BF16)
    kv_sent[...] = kv_out[: kv_sent.shape[0]]


def vision_attend_kernel(where, q, kv, mixed, probs, bias):
    width = q.shape[1]

    @pl.when(where[0] == 0)
    def _():
        keys, queries = bias.shape
        set_bias(bias, text_doc(where, (keys, 1), 0), slot_doc((1, queries), 1))
        attend(q, 0, kv, 0, kv, width, bias, mixed, probs)


def own_attend_kernel(where, q, kv, mixed, probs, bias):
    width = q.shape[1]

    @pl.when(where[0] == 0)
    def _():
        keys, queries = bias.shape
        set_bias(bias, slot_key(where, (keys, 1), 0), text_doc(where, (1, queries), 1))
        attend(q, 0, kv, 0, kv, width, bias, mixed, probs)


def middle_kernel(
    where, x, own_mixed, vision_mixed, pick, gains, shifts, wo, wqkv, ws, wi, wf,
    mixed_hbm, first_low_hbm, unit1_hbm, scale1_hbm, qkv_hbm, self_low_hbm, self_probs_hbm,
    second_low_hbm, unit2_hbm, scale2_hbm, hidden_hbm, slope_hbm, unit3_hbm, scale3_hbm,
    third, third_low, third_sent,
    mixed, first_low, unit1, scale1, qkv, self_low, self_probs, second_low, unit2, scale2, hidden,
    slope, unit3, scale3, first, self_bias, save_sem,
):
    width = x.shape[1]
    rows = x.shape[0]
    packed = vision_mixed.shape[0]
    saves = []

    def save(source, target):
        saves.append(fetch(source, target, save_sem.at[len(saves)]))

    gain = gains[...].astype(F32)
    shift = shifts[...].astype(F32)

    @pl.when(where[0] == 0)
    def _():
        mixed[...] = own_mixed[...]
        set_bias(self_bias, text_doc(where, (rows, 1), 0), text_doc(where, (1, rows), 1))

    @pl.when(where[0] != 0)
    def _():
        mixed[:packed] = vision_mixed[...]
        mixed[packed:] = jnp.zeros((rows - packed, width), BF16)
        set_bias(self_bias, slot_key(where, (rows, 1), 0), slot_doc((1, rows), 1))

    save(mixed, mixed_hbm)
    unit, scale = normalise(x[...].astype(F32) + nn(mixed[...], wo.wait()[...]))
    unit1[...] = unit.astype(BF16)
    scale1[...] = jnp.broadcast_to(scale, scale1.shape)
    first[...] = unit * gain[0:1] + shift[0:1]
    first_low[...] = first[...].astype(BF16)
    save(unit1, unit1_hbm)
    save(scale1, scale1_hbm)
    save(first_low, first_low_hbm)
    qkv[...] = nn(first_low[...], wqkv.wait()[...]).astype(BF16)
    save(qkv, qkv_hbm)
    attend(qkv, 0, qkv, width, qkv, 2 * width, self_bias, self_low, self_probs)
    save(self_low, self_low_hbm)
    save(self_probs, self_probs_hbm)
    unit, scale = normalise(first[...] + nn(self_low[...], ws.wait()[...]))
    unit2[...] = unit.astype(BF16)
    scale2[...] = jnp.broadcast_to(scale, scale2.shape)
    third[...] = unit * gain[1:2] + shift[1:2]
    second_low[...] = third[...].astype(BF16)
    save(unit2, unit2_hbm)
    save(scale2, scale2_hbm)
    save(second_low, second_low_hbm)
    wi = wi.wait()
    wf = wf.wait()
    blocks = hidden.shape[1] // FF_BLOCK
    raw, active = {}, {}
    for turn in range(blocks + 2):
        if turn < blocks:
            raw[turn] = nn(second_low[...], wi[:, turn * FF_BLOCK : (turn + 1) * FF_BLOCK])
        if 0 <= turn - 1 < blocks:
            at = (turn - 1) * FF_BLOCK
            pre = raw.pop(turn - 1)
            below = 0.5 * (1.0 + lax.erf(pre * (2.0**-0.5)))
            density = jnp.exp(pre * pre * -0.5) * 0.3989422804014327
            active[turn - 1] = (pre * below).astype(BF16)
            hidden[:, at : at + FF_BLOCK] = active[turn - 1]
            slope[:, at : at + FF_BLOCK] = (below + pre * density).astype(BF16)
            cols = pl.ds(at, FF_BLOCK)
            save(hidden.at[:, cols], hidden_hbm.at[:, cols])
            save(slope.at[:, cols], slope_hbm.at[:, cols])
        if 0 <= turn - 2:
            at = (turn - 2) * FF_BLOCK
            third[...] += nn(active.pop(turn - 2), wf[at : at + FF_BLOCK, :])
    unit, scale = normalise(third[...])
    unit3[...] = unit.astype(BF16)
    scale3[...] = jnp.broadcast_to(scale, scale3.shape)
    save(unit3, unit3_hbm)
    save(scale3, scale3_hbm)
    third[...] = (unit * gain[2:3] + shift[2:3]) * own_valid(where, rows)
    third_low[...] = third[...].astype(BF16)

    @pl.when(where[0] == 0)
    def _():
        third_sent[...] = nn(pick[...], third_low[...]).astype(BF16)

    @pl.when(where[0] != 0)
    def _():
        third_sent[...] = third_low[:packed]

    for copy in saves:
        copy.wait()


def gate_own_kernel(where, third_low, pick, cot, bias, wg, logits, cot_rows):
    width = third_low.shape[1]
    packed = pick.shape[0]
    logits[...] = nn(third_low[...], wg[:width]) + bias[...].astype(F32)
    given = cot.wait()

    @pl.when(where[0] == 0)
    def _():
        cot_rows[...] = given[...]

    @pl.when(where[0] != 0)
    def _():
        cot_rows[:packed] = nn(pick[...], given[...]).astype(BF16)
        cot_rows[packed:] = jnp.zeros((cot_rows.shape[0] - packed, width), BF16)


def gate_kernel(
    where, third, other, own_logits, cot_rows, pick, pick_t, wg,
    combined, other_low, logit_low, own_part, sent, bias_sum,
):
    rows, width = third.shape
    packed = pick.shape[0]

    @pl.when(where[0] == 0)
    def _():
        other_low[...] = nn(pick_t[...], other[...]).astype(BF16)

    @pl.when(where[0] != 0)
    def _():
        other_low[:packed] = other[...]
        other_low[packed:] = jnp.zeros((rows - packed, width), BF16)

    valid = own_valid(where, rows)
    gate = jax.nn.sigmoid(own_logits[...] + nn(other_low[...], wg[width:]))
    other_rows = other_low[...].astype(F32)
    out_grad = cot_rows[...].astype(F32) * valid
    logit_grad = out_grad * (third[...] - other_rows) * gate * (1.0 - gate)
    bias_sum[...] = jnp.sum(logit_grad, axis=0, keepdims=True)
    logit_low[...] = logit_grad.astype(BF16)
    own_part[...] = nt(logit_low[...], wg[:width]) + out_grad * gate
    partner = (nt(logit_low[...], wg[width:]) + out_grad * (1.0 - gate)).astype(BF16)
    mixed = valid * (gate * third[...] + (1.0 - gate) * other_rows)

    @pl.when(where[0] == 0)
    def _():
        combined[...] = mixed
        sent[...] = nn(pick[...], partner).astype(BF16)

    @pl.when(where[0] != 0)
    def _():
        high = mixed[:packed].astype(BF16)
        rest = (mixed[:packed] - high.astype(F32)).astype(BF16)
        combined[...] = nn(pick_t[...], high) + nn(pick_t[...], rest)
        sent[...] = partner[:packed]


def gate_weight_kernel(split, where, own, other, grad, *outs):
    sent, kept = outs if split else (None,) + outs
    half = own.shape[1]
    full = kept.shape[0] * kept.shape[1] * 2 if split else kept.shape[0]
    for part, left in enumerate((own, other)):
        value = nn(left[...].T, grad[...])
        if split:
            rows = kept.shape[0] * half // full
            put_split(
                split, where[1], value, 0,
                sent.at[pl.ds(part * rows, rows)], kept.at[pl.ds(part * rows, rows)],
            )
        else:
            kept[pl.ds(part * half, half)] = value.astype(BF16)


def third_back_kernel(
    split, where, own_part, returned, pick_t, unit, scale, gains, hidden,
    grad_out, low_out, sums, *rest,
):
    grad = rest[-1]
    kept = rest[-2]
    rows = own_part.shape[0]
    packed = returned.shape[0]
    grad[...] = own_part[...]

    @pl.when(where[0] == 0)
    def _():
        grad[...] += nn(pick_t[...], returned[...])

    @pl.when(where[0] != 0)
    def _():
        grad[:packed] += returned[...].astype(F32)

    value, gain_sum, shift_sum = normalise_back(
        grad[...] * own_valid(where, rows),
        unit.wait()[...].astype(F32),
        scale.wait()[:, 0:1],
        gains[2:3].astype(F32),
    )
    grad_out[...] = value
    low_out[...] = value.astype(BF16)
    sums[0:1] = gain_sum
    sums[1:2] = shift_sum
    hidden = hidden.wait()
    if split:
        sent = rest[0]
        groups, piece = kept.shape[:2]
        even = where[1] == 0
        for group in range(groups):
            left = hidden[:, group * 2 * piece : (group + 1) * 2 * piece].T
            value = nn(left, low_out[...]).astype(BF16)
            kept[group] = jnp.where(even, value[:piece], value[piece:])
            sent[group] = jnp.where(even, value[piece:], value[:piece])
    else:
        for at in range(0, hidden.shape[1], FF_BLOCK):
            left = hidden[:, at : at + FF_BLOCK].T
            kept[at : at + FF_BLOCK] = nn(left, low_out[...]).astype(BF16)


def ffn_back_kernel(
    split, where, third_grad, third_low, wf, slope, second_low, wi, total, *rest
):
    sent, kept, left = rest if split else (None,) + rest
    wf = wf.wait()
    slope = slope.wait()
    total[...] = third_grad[...]
    left[...] = second_low.wait()[...].T
    wi = wi.wait()
    blocks = wi.shape[1] // FF_BLOCK
    back, pre_low = {}, {}
    for turn in range(blocks + 2):
        if turn < blocks:
            back[turn] = nt(third_low[...], wf[turn * FF_BLOCK : (turn + 1) * FF_BLOCK, :])
        if 0 <= turn - 1 < blocks:
            at = (turn - 1) * FF_BLOCK
            pre_low[turn - 1] = (
                back.pop(turn - 1) * slope[:, at : at + FF_BLOCK].astype(F32)
            ).astype(BF16)
        if 0 <= turn - 2:
            at = (turn - 2) * FF_BLOCK
            value = pre_low.pop(turn - 2)
            total[...] += nt(value, wi[:, at : at + FF_BLOCK])
            put_split(split, where[1], nn(left[...], value), at, sent, kept)


def second_back_kernel(total, unit, scale, gains, ws, grad_out, low_out, mixed_grad, sums):
    value, gain_sum, shift_sum = normalise_back(
        total[...], unit.wait()[...].astype(F32), scale.wait()[:, 0:1], gains[1:2].astype(F32)
    )
    grad_out[...] = value
    low_out[...] = value.astype(BF16)
    sums[0:1] = gain_sum
    sums[1:2] = shift_sum
    mixed_grad[...] = nt(low_out[...], ws.wait()[...]).astype(BF16)


def self_back_kernel(
    second_grad, mixed_grad, gains, qkv, self_low, probs, wqkv, unit, scale, wo,
    dqkv, grad_out, low_out, cross, cross_sent, sums,
):
    width = second_grad.shape[1]
    qkv = qkv.wait()
    attend_back(
        qkv, 0, qkv, width, qkv, 2 * width, self_low.wait(), mixed_grad, probs.wait(),
        dqkv, 0, dqkv, width, dqkv, 2 * width,
    )
    value, gain_sum, shift_sum = normalise_back(
        second_grad[...] + nt(dqkv[...], wqkv.wait()[...]),
        unit.wait()[...].astype(F32),
        scale.wait()[:, 0:1],
        gains[0:1].astype(F32),
    )
    grad_out[...] = value
    low_out[...] = value.astype(BF16)
    sums[0:1] = gain_sum
    sums[1:2] = shift_sum
    cross[...] = nt(low_out[...], wo.wait()[...]).astype(BF16)
    cross_sent[...] = cross[: cross_sent.shape[0]]


def self_weight_kernel(
    split, where, dqkv, second_grad, first_grad, first_sums, second_sums, third_sums, bias_sum,
    first_low, self_low, mixed, *outs,
):
    sent, kept, more_sent, more_kept = outs if split else (None, outs[0], None, outs[1])
    width = second_grad.shape[1]
    left = first_low.wait()[...].T
    for part in range(3):
        value = nn(left, dqkv[:, part * width : (part + 1) * width])
        put_split(split, where[1], value, part * width, sent, kept)
    value = nn(self_low.wait()[...].T, second_grad[...])
    put_split(split, where[1], value, 0, more_sent, more_kept)
    value = nn(mixed.wait()[...].T, first_grad[...])
    put_split(split, where[1], value, width, more_sent, more_kept)
    small = jnp.concatenate(
        [first_sums[...], second_sums[...], third_sums[...], bias_sum[...],
         jnp.zeros((121, width), F32)], axis=0,
    )
    put_split(split, where[1], small.T, 2 * width, more_sent, more_kept)


def vision_back_kernel(where, q, kv, mixed, grad, probs, own, sent):
    width = q.shape[1]
    kv, probs = kv.wait(), probs.wait()

    @pl.when(where[0] == 0)
    def _():
        attend_back(q, 0, kv, 0, kv, width, mixed, grad, probs, sent, 0, own, 0, own, width)


def cross_back_kernel(where, q, kv, mixed, grad, probs, own, sent):
    width = kv.shape[1] // 2
    q, mixed, probs = q.wait(), mixed.wait(), probs.wait()

    @pl.when(where[0] == 0)
    def _():
        attend_back(q, 0, kv, 0, kv, width, mixed, grad, probs, own, 0, sent, 0, sent, width)


def cross_weight_kernel(
    split, place, own_query, own_key_value, query, key_value, x, dqkv, left, *outs
):
    sent, kept = outs if split else (None,) + outs
    width = own_query.shape[1]
    packed = query.shape[0]

    @pl.when(place[0] == 0)
    def _():
        dqkv[:, :width] = own_query[...]
        dqkv[:, width:] = own_key_value[...]

    @pl.when(place[0] != 0)
    def _():
        dqkv[:packed, :width] = query[...]
        dqkv[:packed, width:] = key_value[...]
        dqkv[packed:] = jnp.zeros((dqkv.shape[0] - packed, dqkv.shape[1]), BF16)

    left[...] = x.wait()[...].T
    for part in range(2):
        value = nn(left[...], dqkv[:, (1 + part) * width : (2 + part) * width])
        put_split(split, place[1], value, part * width, sent, kept)


def query_weight_kernel(split, place, left, dqkv, *outs):
    sent, kept = outs if split else (None,) + outs
    put_split(split, place[1], nn(left[...], dqkv[:, : left.shape[0]]), 0, sent, kept)


def feature_kernel(where, dqkv, first_grad, pick_t, wq, wkv, out, total):
    width = first_grad.shape[1]
    packed = pick_t.shape[1]
    total[...] = first_grad[...] + nt(dqkv[:, :width], wq.wait()[...])
    total[...] += nt(dqkv[:, width:], wkv.wait()[...])

    @pl.when(where[0] == 0)
    def _():
        out[...] = total[...]

    @pl.when(where[0] != 0)
    def _():
        value = total[:packed]
        high = value.astype(BF16)
        rest = (value - high.astype(F32)).astype(BF16)
        out[...] = nn(pick_t[...], high) + nn(pick_t[...], rest)


def to_partner(shard):
    return lax.ppermute(shard, "stream", [(0, 1), (1, 0)])


def to_language(shard):
    return lax.ppermute(shard, "stream", [(1, 0)])


def to_vision(shard):
    return lax.ppermute(shard, "stream", [(0, 1)])


def swap(shard, bit):
    count = lax.axis_size("docs")
    return lax.ppermute(shard, "docs", [(i, i ^ 1 << bit) for i in range(count)])


def after(value, *others):
    return lax.optimization_barrier((value,) + others)[0] if others else value


def combine_kernel(bit, where, kept, arrived, sent, rest):
    mine = (where[5] >> bit) & 1
    sent[...] = kept[:, 1 - mine] + arrived[:, 1 - mine]
    rest[...] = kept[:, mine] + arrived[:, mine]


def finish_kernel(parts, kept, arrived, *outs):
    for (start, stop), out in zip(parts, outs):
        out[...] = kept[:, start:stop].astype(F32) + arrived[:, start:stop].astype(F32)


def finish_more_kernel(kept, arrived, self_out, cross_out, gain, shift, gate):
    width = self_out.shape[1]
    for at, out in enumerate((self_out, cross_out)):
        cols = slice(at * width, (at + 1) * width)
        out[...] = kept[:, cols].astype(F32) + arrived[:, cols].astype(F32)
    small = (kept[:, 2 * width :].astype(F32) + arrived[:, 2 * width :].astype(F32)).T
    for row in range(3):
        gain[row : row + 1] = small[2 * row : 2 * row + 1]
        shift[row : row + 1] = small[2 * row + 1 : 2 * row + 2]
    gate[...] = small[6:7]


class Summation:
    def __init__(self, parts, first=0):
        index = lax.axis_index("docs")
        count = lax.axis_size("docs")
        self.names = list(range(count.bit_length() - 2, 0, -1))
        bits = list(range(1, count.bit_length() - 1))
        self.order = bits if first == 0 else bits[1:] + bits[:1]
        if len(parts) == 2:
            sent, kept = parts
        else:
            full = parts[0].reshape(count // 2, 2, -1, parts[0].shape[-1])
            core = index & 1
            sent = lax.dynamic_index_in_dim(full, 1 - core, 1, keepdims=False)
            kept = lax.dynamic_index_in_dim(full, core, 1, keepdims=False)
        self.kept = kept
        self.arrived = swap(sent, 0)

    def advance(self, *earlier):
        bit = self.order.pop(0)
        axis = self.names.index(bit)
        ahead, behind = 2**axis, 2 ** (len(self.names) - 1 - axis)
        self.names.pop(axis)
        tail = self.kept.shape[-2:]
        shape = (ahead, 2, behind) + tail
        half = ((ahead, behind) + tail, BF16, VM)
        self.sent, kept = run_kernel(
            functools.partial(combine_kernel, bit), "combine",
            [((), PLACE), (self.kept.reshape(shape), VM),
             (after(self.arrived, *earlier).reshape(shape), VM)],
            [half, half], us=1.0,
        )
        self.kept = kept
        self.arrived = swap(self.sent, bit)

    def last(self, *earlier):
        while self.order:
            self.advance(*earlier)
        shape = self.kept.shape[-2:]
        return [(self.kept.reshape(shape), VM), (after(self.arrived, *earlier).reshape(shape), VM)]

    def finish(self, parts, *earlier):
        operands = self.last(*earlier)
        shape = self.kept.shape[-2:]
        return run_kernel(
            functools.partial(finish_kernel, parts), "finish",
            operands,
            [((shape[0], stop - start), F32, VM) for start, stop in parts], us=1.0,
        )


def body(
    block_features, cotangent, text_counts, visual_counts, w_cross_q, w_cross_kv, w_cross_out,
    w_self_qkv, w_self_out, w_ffn_in, w_ffn_out, w_gate, ln_gain, ln_bias, gate_bias,
):
    feat = block_features[0]
    rows, width = feat.shape
    wq, wkv, wo = w_cross_q[0], w_cross_kv[0], w_cross_out[0]
    wqkv, ws = w_self_qkv[0], w_self_out[0]
    wi, wf, wg = w_ffn_in[0], w_ffn_out[0], w_gate[0]
    gains, shifts = ln_gain[0], ln_bias[0]
    hidden_width = wi.shape[1]
    count = lax.axis_size("docs")
    groups = count // 2
    split = (width // count) % 16 == 0
    packed = text_counts.shape[1] * SLOT
    heads = width // HD
    where = (text_counts, visual_counts)
    here = ()
    dma = pltpu.SemaphoreType.DMA
    low = ((rows, width), BF16, VM)
    wide = ((rows, width), F32, VM)
    sums = ((2, width), F32, VM)
    few = ((packed, width), BF16, VM)

    def weight_outs(total_rows, columns):
        if split:
            shape = (groups, total_rows // count, columns)
            return [(shape, BF16, VM), (shape, BF16, VM)]
        return [((total_rows, columns), BF16, VM)]

    parts = 2 if split else 1
    x, q, q_sent, pick, pick_t = run_kernel(
        query_kernel, "query",
        [(where, PLACE), (feat, LAZY), (wq, LAZY)],
        [low, low, few, ((packed, rows), BF16, VM), ((rows, packed), BF16, VM)],
        spare=48 << 20,
    )
    vision_q = to_language(q_sent)
    kv, kv_sent = run_kernel(
        key_value_kernel, "key_value",
        [(after(x, q_sent), VM), (wkv, VM)],
        [((rows, 2 * width), BF16, VM), ((packed, 2 * width), BF16, VM)],
    )
    vision_kv = to_language(kv_sent)
    vision_mixed, vision_probs = run_kernel(
        vision_attend_kernel, "vision_attend",
        [(where, PLACE), (vision_q, VM), (after(kv, kv_sent), VM)],
        [few, ((heads, rows, packed), BF16, VM)],
        [VM((rows, packed), F32)],
    )
    vision_mixed_here = to_vision(vision_mixed)
    own_mixed, cross_probs = run_kernel(
        own_attend_kernel, "own_attend",
        [(where, PLACE), (q, VM), (after(vision_kv, vision_mixed), VM)],
        [low, ((heads, packed, rows), BF16, VM)],
        [VM((packed, rows), F32)],
    )

    def state(*shape, kind=BF16):
        return (shape, kind, HBM)

    full = state(rows, width)
    lane = state(rows, 128, kind=F32)
    saved = [
        full, full, full, lane, state(rows, 3 * width), full, state(heads, rows, rows), full, full,
        lane, state(rows, hidden_width), state(rows, hidden_width), full, lane,
    ]
    (
        mixed, first_low, unit1, scale1, qkv, self_low, self_probs, second_low, unit2, scale2,
        hidden, slope, unit3, scale3, third, third_low, third_sent,
    ) = run_kernel(
        middle_kernel, "middle",
        [(where, PLACE), (x, VM), (own_mixed, VM), (after(vision_mixed_here, own_mixed), VM),
         (pick, VM), (gains, VM), (shifts, VM)] + [(w, LAZY) for w in (wo, wqkv, ws, wi, wf)],
        saved + [wide, low, few],
        [VM(shape, kind) for shape, kind, _ in saved]
        + [VM((rows, width), F32), VM((rows, rows), F32),
           dma((len(saved) - 2 + 2 * (hidden_width // FF_BLOCK),))],
        spare=VMEM_LIMIT,
    )
    other = to_partner(third_sent)
    own_logits, cot_rows = run_kernel(
        gate_own_kernel, "gate_own",
        [(here, PLACE), (after(third_low, third_sent), VM), (pick, VM), (cotangent[0], LAZY),
         (gate_bias, VM), (wg, VM)],
        [wide, low],
    )
    combined, other_low, logit_low, own_part, partner_sent, bias_sum = run_kernel(
        gate_kernel, "gate",
        [(where, PLACE), (third, VM), (after(other, own_logits), VM), (own_logits, VM),
         (cot_rows, VM), (pick, VM), (pick_t, VM), (wg, VM)],
        [wide, low, low, wide, few, ((1, width), F32, VM)],
    )
    returned = to_partner(partner_sent)
    gate_parts = run_kernel(
        functools.partial(gate_weight_kernel, split), "gate_weight",
        [(here, PLACE), (third_low, VM), (other_low, VM), (after(logit_low, partner_sent), VM)],
        weight_outs(2 * width, width),
    )
    gate_sum = Summation(gate_parts, 0)
    gate_sum.advance()
    third_back = run_kernel(
        functools.partial(third_back_kernel, split), "third_back",
        [(where, PLACE), (own_part, VM), (after(returned, gate_sum.sent), VM), (pick_t, VM),
         (unit3, LAZY), (scale3, LAZY), (gains, VM), (hidden, LAZY)],
        [wide, low, sums] + weight_outs(hidden_width, width),
        [VM((rows, width), F32)],
    )
    third_grad, third_grad_low, third_sums = third_back[:3]
    out_sum = Summation(third_back[3:], 0)
    ffn_back = run_kernel(
        functools.partial(ffn_back_kernel, split), "ffn_back",
        [(here, PLACE), (third_grad, VM), (after(third_grad_low, *third_back[3:]), VM), (wf, LAZY),
         (slope, LAZY), (second_low, LAZY), (wi, LAZY)],
        [wide] + weight_outs(width, hidden_width),
        [VM((width, rows), BF16)],
    )
    in_sum = Summation(ffn_back[1:], 0)
    out_sum.advance(ffn_back[0])
    second_grad, second_grad_low, mixed_grad, second_sums = run_kernel(
        second_back_kernel, "second_back",
        [(after(ffn_back[0], out_sum.sent, *ffn_back[1:]), VM), (unit2, LAZY), (scale2, LAZY),
         (gains, VM), (ws, LAZY)],
        [wide, low, low, sums],
    )
    in_sum.advance(second_sums)
    dqkv, first_grad, first_grad_low, cross_grad, cross_grad_sent, first_sums = run_kernel(
        self_back_kernel, "self_back",
        [(second_grad, VM), (after(mixed_grad, in_sum.sent), VM), (gains, VM),
         (qkv, LAZY), (self_low, LAZY), (self_probs, LAZY), (wqkv, LAZY), (unit1, LAZY),
         (scale1, LAZY), (wo, LAZY)],
        [((rows, 3 * width), BF16, VM), wide, low, low, few, sums],
    )
    vision_grad = to_language(cross_grad_sent)
    gate_sum.advance(first_sums)
    out_sum.advance(gate_sum.sent)
    self_parts = run_kernel(
        functools.partial(self_weight_kernel, split), "self_weight",
        [(here, PLACE), (after(dqkv, cross_grad_sent, out_sum.sent), VM), (second_grad_low, VM),
         (first_grad_low, VM), (first_sums, VM), (second_sums, VM), (third_sums, VM),
         (bias_sum, VM), (first_low, LAZY), (self_low, LAZY), (mixed, LAZY)],
        weight_outs(width, 3 * width) + weight_outs(width, 2 * width + 128),
    )
    self_sum = Summation(self_parts[:parts], 0)
    more_sum = Summation(self_parts[parts:], 0)
    gate_sum.advance(*self_parts)
    own_key_value, query_sent = run_kernel(
        vision_back_kernel, "vision_back",
        [(here, PLACE), (vision_q, VM), (kv, LAZY), (vision_mixed, VM),
         (after(vision_grad, gate_sum.sent, *self_parts), VM), (vision_probs, LAZY)],
        [((rows, 2 * width), BF16, VM), few],
    )
    query_here = to_vision(query_sent)
    self_sum.advance(query_sent)
    more_sum.advance(self_sum.sent)
    own_query, key_value_sent = run_kernel(
        cross_back_kernel, "cross_back",
        [(here, PLACE), (q, LAZY), (vision_kv, VM), (mixed, LAZY),
         (after(cross_grad, query_here, more_sum.sent), VM),
         (cross_probs, LAZY)],
        [low, ((packed, 2 * width), BF16, VM)],
    )
    key_value_here = to_vision(key_value_sent)
    in_sum.advance(key_value_sent)
    out_sum.advance(in_sum.sent)
    (gate_grad,) = gate_sum.finish([(0, width)], out_sum.sent)
    self_sum.advance(gate_grad)
    cross_out = run_kernel(
        functools.partial(cross_weight_kernel, split), "cross_weight",
        [(here, PLACE), (own_query, VM), (own_key_value, VM), (query_here, VM),
         (after(key_value_here, self_sum.sent), VM), (x, LAZY)],
        [((rows, 3 * width), BF16, VM), ((width, rows), BF16, VM)]
        + weight_outs(width, 2 * width),
    )
    dcross, left = cross_out[:2]
    cross_sum = Summation(cross_out[2:], 0)
    (feature_grad,) = run_kernel(
        feature_kernel, "feature",
        [(here, PLACE), (after(dcross, *cross_out[2:]), VM), (first_grad, VM), (pick_t, VM),
         (wq, LAZY), (wkv, LAZY)],
        [wide],
        [VM((rows, width), F32)],
    )
    cross_sum.advance(feature_grad)
    (ffn_out_grad,) = out_sum.finish([(0, width)], cross_sum.sent)
    in_sum.advance(ffn_out_grad)
    last_parts = run_kernel(
        functools.partial(query_weight_kernel, split), "query_weight",
        [(here, PLACE), (left, VM), (after(dcross, in_sum.sent), VM)],
        weight_outs(width, width),
    )
    last_sum = Summation(last_parts, 0)
    self_sum.advance(*last_parts)
    last_sum.advance(self_sum.sent)
    more_sum.advance(last_sum.sent)
    cross_sum.advance(more_sum.sent)
    (ffn_in_grad,) = in_sum.finish([(0, hidden_width)], cross_sum.sent)
    last_sum.advance(ffn_in_grad)
    (self_qkv_grad,) = self_sum.finish([(0, 3 * width)], last_sum.sent)
    more_sum.advance(self_qkv_grad)
    cross_sum.advance(more_sum.sent)
    last_sum.advance(cross_sum.sent)
    if split:
        piece = width // count
        self_out_grad, cross_out_grad, gain_grad, shift_grad, gate_bias_grad = run_kernel(
            finish_more_kernel, "finish_more", more_sum.last(last_sum.sent),
            [((piece, width), F32, VM)] * 2 + [((3, piece), F32, VM)] * 2 + [((1, piece), F32, VM)],
            us=1.0,
        )
    else:
        self_out_grad, cross_out_grad, small = more_sum.finish(
            [(0, width), (width, 2 * width), (2 * width, 2 * width + 128)], last_sum.sent
        )
        small = small[:, :7].T
        gain_grad, shift_grad, gate_bias_grad = small[0:6:2], small[1:6:2], small[6:7]
    (cross_kv_grad,) = cross_sum.finish([(0, 2 * width)], self_out_grad)
    (cross_q_grad,) = last_sum.finish([(0, width)])
    return (
        combined[None],
        feature_grad[None],
        cross_q_grad[None],
        cross_kv_grad[None],
        cross_out_grad[None],
        self_qkv_grad[None],
        self_out_grad[None],
        ffn_in_grad[None],
        ffn_out_grad[None],
        gate_grad[None],
        gain_grad[None],
        shift_grad[None],
        gate_bias_grad,
    )


def solution(mesh):
    rows = P("stream", "docs", None)
    weight = P("stream", None, None)
    return jax.shard_map(
        body,
        mesh=mesh,
        in_specs=(rows, rows, P("docs", None), P("docs", None)) + (weight,) * 10
        + (P("stream", None),),
        out_specs=(rows,) * 10 + (P("stream", None, "docs"),) * 2 + (P("stream", "docs"),),
        check_vma=False,
    )
```

```python
import functools

import jax
import jax.numpy as jnp
from jax import lax
from jax.experimental import pallas as pl
from jax.experimental.pallas import tpu as pltpu
from jax.sharding import PartitionSpec as P

HD = 64
PAIR = 2 * HD
SLOT = 96
FF_BLOCK = 512
VMEM_LIMIT = 60 << 20
F32 = jnp.float32
BF16 = jnp.bfloat16
norm_epsilon = 1e-06
masked_value = -1e30

VM = pltpu.VMEM
SM = pltpu.SMEM
HBM = pltpu.HBM
LAZY = "lazy"
PLACE = "place"


def nn(left, right):
    return lax.dot_general(left, right, (((1,), (0,)), ((), ())), preferred_element_type=F32)


def nt(left, right):
    return lax.dot_general(left, right, (((1,), (1,)), ((), ())), preferred_element_type=F32)


def padded_bytes(shape, dtype):
    size = jnp.dtype(dtype).itemsize
    shape = (1,) * (2 - len(shape)) + tuple(shape)
    tile = 32 // size
    total = -(-shape[-1] // 128) * 128 * -(-shape[-2] // tile) * tile * size
    for extent in shape[:-2]:
        total *= extent
    return total


class Arriving:
    def __init__(self, source, target, sem):
        self.copy, self.ref = fetch(source, target, sem), target

    def wait(self):
        if self.copy is not None:
            self.copy.wait()
            self.copy = None
        return self.ref


class Place:
    def __init__(self, text=None, visual=None):
        self.text, self.visual = text, visual

    def __getitem__(self, what):
        if what == 0:
            return lax.axis_index("stream")
        if what == 1:
            return lax.axis_index("docs") & 1
        if what == 5:
            return lax.axis_index("docs")
        return self.text[0, 0] if what == 2 else self.visual[0, what - 3]


def run_kernel(kernel, name, ins, outs, scratch=(), us=5.0, spare=6 << 20):
    counts = ()
    place = ins[0][1] is PLACE
    if place:
        counts, ins = ins[0][0], ins[1:]
    lazy = [at for at, (_, space) in enumerate(ins) if space is LAZY]
    scratch = list(scratch)
    own = len(scratch)
    scratch += [VM(ins[at][0].shape, ins[at][0].dtype) for at in lazy]
    if lazy:
        scratch.append(pltpu.SemaphoreType.DMA((len(lazy),)))
    need = sum(padded_bytes(array.shape, array.dtype) for array, space in ins if space is VM)
    need += sum(padded_bytes(shape, dtype) for shape, dtype, space in outs if space is VM)
    need += sum(
        padded_bytes(ref.shape, ref.dtype) for ref in scratch if hasattr(ref, "memory_space")
        and ref.memory_space == VM
    )

    def wrapped(*refs):
        front = (Place(*refs[: len(counts)]),) if place else ()
        refs = refs[len(counts) :]
        first = len(ins) + len(outs)
        operands = list(refs[: len(ins)])
        extra = refs[first + own :]
        for slot, at in enumerate(lazy):
            operands[at] = Arriving(operands[at], extra[slot], extra[-1].at[slot])
        kernel(*front, *operands, *refs[len(ins) : first + own])

    return pl.pallas_call(
        wrapped,
        name=name,
        in_specs=[pl.BlockSpec(memory_space=SM)] * len(counts)
        + [pl.BlockSpec(memory_space=HBM if space is LAZY else space) for _, space in ins],
        out_specs=[pl.BlockSpec(memory_space=space) for _, _, space in outs],
        out_shape=[jax.ShapeDtypeStruct(shape, dtype) for shape, dtype, _ in outs],
        scratch_shapes=scratch,
        compiler_params=pltpu.CompilerParams(vmem_limit_bytes=min(VMEM_LIMIT, need + spare)),
        cost_estimate=pl.CostEstimate(
            flops=int(us * 30e9), bytes_accessed=1000, transcendentals=0
        ),
    )(*counts, *[array for array, _ in ins])


def fetch(source, target, sem):
    copy = pltpu.make_async_copy(source, target, sem)
    copy.start()
    return copy


def normalise(resid):
    center = resid - jnp.mean(resid, axis=-1, keepdims=True)
    scale = lax.rsqrt(jnp.mean(center * center, axis=-1, keepdims=True) + norm_epsilon)
    return center * scale, scale


def normalise_back(grad, unit, scale, gain):
    gain_sum = jnp.sum(grad * unit, axis=0, keepdims=True)
    shift_sum = jnp.sum(grad, axis=0, keepdims=True)
    scaled = grad * gain
    first = jnp.mean(scaled, axis=-1, keepdims=True)
    second = jnp.mean(scaled * unit, axis=-1, keepdims=True)
    return scale * (scaled - first - unit * second), gain_sum, shift_sum


def attend(q_ref, q_at, k_ref, k_at, v_ref, v_at, bias_ref, out_ref, probs_ref):
    heads = out_ref.shape[1] // HD
    first = lax.broadcasted_iota(jnp.int32, (k_ref.shape[0], PAIR), 1) < HD
    queries, values, scores, probs, mixed = {}, {}, {}, {}, {}
    for turn in range(heads + 2):
        if turn < heads:
            pair, head = divmod(turn, 2)
            at = pair * PAIR
            if head == 0:
                queries[pair] = q_ref[:, q_at + at : q_at + at + PAIR] * jnp.asarray(
                    HD**-0.5, BF16
                )
            keys = k_ref[:, k_at + at : k_at + at + PAIR]
            zero = jnp.zeros_like(keys)
            own = jnp.where(first, keys, zero) if head == 0 else jnp.where(first, zero, keys)
            scores[turn] = nt(own, queries[pair])
        if 0 <= turn - 1 < heads:
            at = turn - 1
            raw = scores.pop(at) + bias_ref[...]
            shifted = jnp.exp(raw - jnp.max(raw, axis=0, keepdims=True))
            probs[at] = (shifted * (1.0 / jnp.sum(shifted, axis=0, keepdims=True))).astype(BF16)
            probs_ref[at] = probs[at]
        if 0 <= turn - 2:
            pair, head = divmod(turn - 2, 2)
            at = pair * PAIR
            if head == 0:
                values[pair] = v_ref[:, v_at + at : v_at + at + PAIR].T
            mixed[head] = nn(values[pair][head * HD : (head + 1) * HD], probs.pop(turn - 2))
            if head == 1:
                out_ref[:, at : at + PAIR] = (
                    jnp.concatenate([mixed[0], mixed[1]], axis=0).astype(BF16).T
                )


def attend_back(
    q_ref, q_at, k_ref, k_at, v_ref, v_at, mixed_ref, grad_ref, probs_ref,
    dq_ref, dq_at, dk_ref, dk_at, dv_ref, dv_at,
):
    heads = grad_ref.shape[1] // HD
    scale = HD**-0.5
    first = lax.broadcasted_iota(jnp.int32, (k_ref.shape[0], PAIR), 1) < HD

    def columns(ref, start, pair):
        return ref[:, start + pair * PAIR : start + (pair + 1) * PAIR]

    grads_t, inner, prob_grads, score_grads = {}, {}, {}, {}
    key_grads, value_grads, query_grads = {}, {}, {}
    for turn in range(heads + 2):
        if turn < heads:
            pair, head = divmod(turn, 2)
            if head == 0:
                grads_t[pair] = columns(grad_ref, 0, pair).T
                inner[pair] = grads_t[pair].astype(F32) * columns(mixed_ref, 0, pair).T.astype(F32)
            values = columns(v_ref, v_at, pair)
            zero = jnp.zeros_like(values)
            own = jnp.where(first, values, zero) if head == 0 else jnp.where(first, zero, values)
            prob_grads[turn] = nn(own, grads_t[pair])
        if 0 <= turn - 1 < heads:
            pair, head = divmod(turn - 1, 2)
            weighed = jnp.sum(inner[pair][head * HD : (head + 1) * HD], axis=0, keepdims=True)
            score_grads[turn - 1] = (
                probs_ref[turn - 1].astype(F32) * (prob_grads.pop(turn - 1) - weighed)
            ).astype(BF16)
        if 0 <= turn - 2:
            pair, head = divmod(turn - 2, 2)
            score_grad = score_grads.pop(turn - 2)
            key_grads[head] = nn(score_grad, columns(q_ref, q_at, pair))
            value_grads[head] = nn(probs_ref[turn - 2], columns(grad_ref, 0, pair))
            keys_t = columns(k_ref, k_at, pair).T
            query_grads[head] = nn(keys_t[head * HD : (head + 1) * HD], score_grad)
            if head == 1:
                at = pair * PAIR
                dk_ref[:, dk_at + at : dk_at + at + PAIR] = (
                    jnp.where(first, key_grads[0], key_grads[1]) * scale
                ).astype(BF16)
                dv_ref[:, dv_at + at : dv_at + at + PAIR] = jnp.where(
                    first, value_grads[0], value_grads[1]
                ).astype(BF16)
                dq_ref[:, dq_at + at : dq_at + at + PAIR] = (
                    (jnp.concatenate([query_grads[0], query_grads[1]], axis=0) * scale)
                    .astype(BF16)
                    .T
                )


def iota(shape, dim):
    return lax.broadcasted_iota(jnp.int32, shape, dim)


def text_doc(where, shape, dim):
    return (iota(shape, dim) >= where[2]).astype(jnp.int32)


def slot_doc(shape, dim):
    row = iota(shape, dim)
    return (row >= SLOT).astype(jnp.int32) + (row >= 2 * SLOT).astype(jnp.int32)


def slot_seen(where, shape, dim):
    row = iota(shape, dim)
    doc = slot_doc(shape, dim)
    count = jnp.where(doc == 0, where[3], jnp.where(doc == 1, where[4], 0))
    return row - doc * SLOT < count


def slot_key(where, shape, dim):
    return jnp.where(slot_seen(where, shape, dim), slot_doc(shape, dim), -1)


def picked(where, shape, packed_dim):
    doc = slot_doc(shape, packed_dim)
    place = iota(shape, packed_dim) - doc * SLOT + doc * where[2]
    same = (place == iota(shape, 1 - packed_dim)) & slot_seen(where, shape, packed_dim)
    return jnp.where(same, 1.0, 0.0).astype(BF16)


def set_bias(bias_ref, key_doc, query_doc):
    bias_ref[...] = jnp.where(key_doc == query_doc, 0.0, masked_value)


def own_valid(where, rows):
    seen = slot_seen(where, (rows, 1), 0)
    return jnp.where(seen | (where[0] == 0), 1.0, 0.0).astype(F32)


def put_split(split, core, value, at, sent_ref, kept_ref):
    cols = slice(at, at + value.shape[1])
    if not split:
        kept_ref[:, cols] = value.astype(BF16)
        return
    groups, piece = kept_ref.shape[:2]
    pieces = value.reshape(groups, 2, piece, value.shape[1]).astype(BF16)
    even = core == 0
    kept_ref[:, :, cols] = jnp.where(even, pieces[:, 0], pieces[:, 1])
    sent_ref[:, :, cols] = jnp.where(even, pieces[:, 1], pieces[:, 0])


def query_kernel(where, feat, wq, x_out, q_out, q_sent, pick, pick_t):
    packed = pick.shape[0]
    pick[...] = picked(where, pick.shape, 0)
    pick_t[...] = picked(where, pick_t.shape, 1)
    rows = feat.wait()

    @pl.when(where[0] == 0)
    def _():
        x_out[...] = rows[...]

    @pl.when(where[0] != 0)
    def _():
        x_out[:packed] = nn(pick[...], rows[...]).astype(BF16)
        x_out[packed:] = jnp.zeros((x_out.shape[0] - packed, x_out.shape[1]), BF16)

    q_out[...] = nn(x_out[...], wq.wait()[...]).astype(BF16)
    q_sent[...] = q_out[:packed]


def key_value_kernel(x, w, kv_out, kv_sent):
    kv_out[...] = nn(x[...], w[...]).astype(BF16)
    kv_sent[...] = kv_out[: kv_sent.shape[0]]


def vision_attend_kernel(where, q, kv, mixed, probs, bias):
    width = q.shape[1]

    @pl.when(where[0] == 0)
    def _():
        keys, queries = bias.shape
        set_bias(bias, text_doc(where, (keys, 1), 0), slot_doc((1, queries), 1))
        attend(q, 0, kv, 0, kv, width, bias, mixed, probs)


def own_attend_kernel(where, q, kv, mixed, probs, bias):
    width = q.shape[1]

    @pl.when(where[0] == 0)
    def _():
        keys, queries = bias.shape
        set_bias(bias, slot_key(where, (keys, 1), 0), text_doc(where, (1, queries), 1))
        attend(q, 0, kv, 0, kv, width, bias, mixed, probs)


def middle_kernel(
    where, x, own_mixed, vision_mixed, pick, gains, shifts, wo, wqkv, ws, wi, wf,
    mixed_hbm, first_low_hbm, unit1_hbm, scale1_hbm, qkv_hbm, self_low_hbm, self_probs_hbm,
    second_low_hbm, unit2_hbm, scale2_hbm, hidden_hbm, slope_hbm, unit3_hbm, scale3_hbm,
    third, third_low, third_sent,
    mixed, first_low, unit1, scale1, qkv, self_low, self_probs, second_low, unit2, scale2, hidden,
    slope, unit3, scale3, first, self_bias, save_sem,
):
    width = x.shape[1]
    rows = x.shape[0]
    packed = vision_mixed.shape[0]
    saves = []

    def save(source, target):
        saves.append(fetch(source, target, save_sem.at[len(saves)]))

    gain = gains[...].astype(F32)
    shift = shifts[...].astype(F32)

    @pl.when(where[0] == 0)
    def _():
        mixed[...] = own_mixed[...]
        set_bias(self_bias, text_doc(where, (rows, 1), 0), text_doc(where, (1, rows), 1))

    @pl.when(where[0] != 0)
    def _():
        mixed[:packed] = vision_mixed[...]
        mixed[packed:] = jnp.zeros((rows - packed, width), BF16)
        set_bias(self_bias, slot_key(where, (rows, 1), 0), slot_doc((1, rows), 1))

    save(mixed, mixed_hbm)
    unit, scale = normalise(x[...].astype(F32) + nn(mixed[...], wo.wait()[...]))
    unit1[...] = unit.astype(BF16)
    scale1[...] = jnp.broadcast_to(scale, scale1.shape)
    first[...] = unit * gain[0:1] + shift[0:1]
    first_low[...] = first[...].astype(BF16)
    save(unit1, unit1_hbm)
    save(scale1, scale1_hbm)
    save(first_low, first_low_hbm)
    qkv[...] = nn(first_low[...], wqkv.wait()[...]).astype(BF16)
    save(qkv, qkv_hbm)
    attend(qkv, 0, qkv, width, qkv, 2 * width, self_bias, self_low, self_probs)
    save(self_low, self_low_hbm)
    save(self_probs, self_probs_hbm)
    unit, scale = normalise(first[...] + nn(self_low[...], ws.wait()[...]))
    unit2[...] = unit.astype(BF16)
    scale2[...] = jnp.broadcast_to(scale, scale2.shape)
    third[...] = unit * gain[1:2] + shift[1:2]
    second_low[...] = third[...].astype(BF16)
    save(unit2, unit2_hbm)
    save(scale2, scale2_hbm)
    save(second_low, second_low_hbm)
    wi = wi.wait()
    wf = wf.wait()
    blocks = hidden.shape[1] // FF_BLOCK
    raw, active = {}, {}
    for turn in range(blocks + 2):
        if turn < blocks:
            raw[turn] = nn(second_low[...], wi[:, turn * FF_BLOCK : (turn + 1) * FF_BLOCK])
        if 0 <= turn - 1 < blocks:
            at = (turn - 1) * FF_BLOCK
            pre = raw.pop(turn - 1)
            below = 0.5 * (1.0 + lax.erf(pre * (2.0**-0.5)))
            density = jnp.exp(pre * pre * -0.5) * 0.3989422804014327
            active[turn - 1] = (pre * below).astype(BF16)
            hidden[:, at : at + FF_BLOCK] = active[turn - 1]
            slope[:, at : at + FF_BLOCK] = (below + pre * density).astype(BF16)
            cols = pl.ds(at, FF_BLOCK)
            save(hidden.at[:, cols], hidden_hbm.at[:, cols])
            save(slope.at[:, cols], slope_hbm.at[:, cols])
        if 0 <= turn - 2:
            at = (turn - 2) * FF_BLOCK
            third[...] += nn(active.pop(turn - 2), wf[at : at + FF_BLOCK, :])
    unit, scale = normalise(third[...])
    unit3[...] = unit.astype(BF16)
    scale3[...] = jnp.broadcast_to(scale, scale3.shape)
    save(unit3, unit3_hbm)
    save(scale3, scale3_hbm)
    third[...] = (unit * gain[2:3] + shift[2:3]) * own_valid(where, rows)
    third_low[...] = third[...].astype(BF16)

    @pl.when(where[0] == 0)
    def _():
        third_sent[...] = nn(pick[...], third_low[...]).astype(BF16)

    @pl.when(where[0] != 0)
    def _():
        third_sent[...] = third_low[:packed]

    for copy in saves:
        copy.wait()


def gate_own_kernel(where, third_low, pick, cot, bias, wg, logits, cot_rows):
    width = third_low.shape[1]
    packed = pick.shape[0]
    logits[...] = nn(third_low[...], wg[:width]) + bias[...].astype(F32)
    given = cot.wait()

    @pl.when(where[0] == 0)
    def _():
        cot_rows[...] = given[...]

    @pl.when(where[0] != 0)
    def _():
        cot_rows[:packed] = nn(pick[...], given[...]).astype(BF16)
        cot_rows[packed:] = jnp.zeros((cot_rows.shape[0] - packed, width), BF16)


def gate_kernel(
    where, third, other, own_logits, cot_rows, pick, pick_t, wg,
    combined, other_low, logit_low, own_part, sent, bias_sum,
):
    rows, width = third.shape
    packed = pick.shape[0]

    @pl.when(where[0] == 0)
    def _():
        other_low[...] = nn(pick_t[...], other[...]).astype(BF16)

    @pl.when(where[0] != 0)
    def _():
        other_low[:packed] = other[...]
        other_low[packed:] = jnp.zeros((rows - packed, width), BF16)

    valid = own_valid(where, rows)
    gate = jax.nn.sigmoid(own_logits[...] + nn(other_low[...], wg[width:]))
    other_rows = other_low[...].astype(F32)
    out_grad = cot_rows[...].astype(F32) * valid
    logit_grad = out_grad * (third[...] - other_rows) * gate * (1.0 - gate)
    bias_sum[...] = jnp.sum(logit_grad, axis=0, keepdims=True)
    logit_low[...] = logit_grad.astype(BF16)
    own_part[...] = nt(logit_low[...], wg[:width]) + out_grad * gate
    partner = (nt(logit_low[...], wg[width:]) + out_grad * (1.0 - gate)).astype(BF16)
    mixed = valid * (gate * third[...] + (1.0 - gate) * other_rows)

    @pl.when(where[0] == 0)
    def _():
        combined[...] = mixed
        sent[...] = nn(pick[...], partner).astype(BF16)

    @pl.when(where[0] != 0)
    def _():
        high = mixed[:packed].astype(BF16)
        rest = (mixed[:packed] - high.astype(F32)).astype(BF16)
        combined[...] = nn(pick_t[...], high) + nn(pick_t[...], rest)
        sent[...] = partner[:packed]


def gate_weight_kernel(split, where, own, other, grad, *outs):
    sent, kept = outs if split else (None,) + outs
    half = own.shape[1]
    full = kept.shape[0] * kept.shape[1] * 2 if split else kept.shape[0]
    for part, left in enumerate((own, other)):
        value = nn(left[...].T, grad[...])
        if split:
            rows = kept.shape[0] * half // full
            put_split(
                split, where[1], value, 0,
                sent.at[pl.ds(part * rows, rows)], kept.at[pl.ds(part * rows, rows)],
            )
        else:
            kept[pl.ds(part * half, half)] = value.astype(BF16)


def third_back_kernel(
    split, where, own_part, returned, pick_t, unit, scale, gains, hidden,
    grad_out, low_out, sums, *rest,
):
    grad = rest[-1]
    kept = rest[-2]
    rows = own_part.shape[0]
    packed = returned.shape[0]
    grad[...] = own_part[...]

    @pl.when(where[0] == 0)
    def _():
        grad[...] += nn(pick_t[...], returned[...])

    @pl.when(where[0] != 0)
    def _():
        grad[:packed] += returned[...].astype(F32)

    value, gain_sum, shift_sum = normalise_back(
        grad[...] * own_valid(where, rows),
        unit.wait()[...].astype(F32),
        scale.wait()[:, 0:1],
        gains[2:3].astype(F32),
    )
    grad_out[...] = value
    low_out[...] = value.astype(BF16)
    sums[0:1] = gain_sum
    sums[1:2] = shift_sum
    hidden = hidden.wait()
    if split:
        sent = rest[0]
        groups, piece = kept.shape[:2]
        even = where[1] == 0
        for group in range(groups):
            left = hidden[:, group * 2 * piece : (group + 1) * 2 * piece].T
            value = nn(left, low_out[...]).astype(BF16)
            kept[group] = jnp.where(even, value[:piece], value[piece:])
            sent[group] = jnp.where(even, value[piece:], value[:piece])
    else:
        for at in range(0, hidden.shape[1], FF_BLOCK):
            left = hidden[:, at : at + FF_BLOCK].T
            kept[at : at + FF_BLOCK] = nn(left, low_out[...]).astype(BF16)


def ffn_back_kernel(
    split, where, third_grad, third_low, wf, slope, second_low, wi, total, *rest
):
    sent, kept, left = rest if split else (None,) + rest
    wf = wf.wait()
    slope = slope.wait()
    total[...] = third_grad[...]
    left[...] = second_low.wait()[...].T
    wi = wi.wait()
    blocks = wi.shape[1] // FF_BLOCK
    back, pre_low = {}, {}
    for turn in range(blocks + 2):
        if turn < blocks:
            back[turn] = nt(third_low[...], wf[turn * FF_BLOCK : (turn + 1) * FF_BLOCK, :])
        if 0 <= turn - 1 < blocks:
            at = (turn - 1) * FF_BLOCK
            pre_low[turn - 1] = (
                back.pop(turn - 1) * slope[:, at : at + FF_BLOCK].astype(F32)
            ).astype(BF16)
        if 0 <= turn - 2:
            at = (turn - 2) * FF_BLOCK
            value = pre_low.pop(turn - 2)
            total[...] += nt(value, wi[:, at : at + FF_BLOCK])
            put_split(split, where[1], nn(left[...], value), at, sent, kept)


def second_back_kernel(total, unit, scale, gains, ws, grad_out, low_out, mixed_grad, sums):
    value, gain_sum, shift_sum = normalise_back(
        total[...], unit.wait()[...].astype(F32), scale.wait()[:, 0:1], gains[1:2].astype(F32)
    )
    grad_out[...] = value
    low_out[...] = value.astype(BF16)
    sums[0:1] = gain_sum
    sums[1:2] = shift_sum
    mixed_grad[...] = nt(low_out[...], ws.wait()[...]).astype(BF16)


def self_back_kernel(
    second_grad, mixed_grad, gains, qkv, self_low, probs, wqkv, unit, scale, wo,
    dqkv, grad_out, low_out, cross, cross_sent, sums,
):
    width = second_grad.shape[1]
    qkv = qkv.wait()
    attend_back(
        qkv, 0, qkv, width, qkv, 2 * width, self_low.wait(), mixed_grad, probs.wait(),
        dqkv, 0, dqkv, width, dqkv, 2 * width,
    )
    value, gain_sum, shift_sum = normalise_back(
        second_grad[...] + nt(dqkv[...], wqkv.wait()[...]),
        unit.wait()[...].astype(F32),
        scale.wait()[:, 0:1],
        gains[0:1].astype(F32),
    )
    grad_out[...] = value
    low_out[...] = value.astype(BF16)
    sums[0:1] = gain_sum
    sums[1:2] = shift_sum
    cross[...] = nt(low_out[...], wo.wait()[...]).astype(BF16)
    cross_sent[...] = cross[: cross_sent.shape[0]]


def self_weight_kernel(
    split, where, dqkv, second_grad, first_grad, first_sums, second_sums, third_sums, bias_sum,
    first_low, self_low, mixed, *outs,
):
    sent, kept, more_sent, more_kept = outs if split else (None, outs[0], None, outs[1])
    width = second_grad.shape[1]
    left = first_low.wait()[...].T
    for part in range(3):
        value = nn(left, dqkv[:, part * width : (part + 1) * width])
        put_split(split, where[1], value, part * width, sent, kept)
    value = nn(self_low.wait()[...].T, second_grad[...])
    put_split(split, where[1], value, 0, more_sent, more_kept)
    value = nn(mixed.wait()[...].T, first_grad[...])
    put_split(split, where[1], value, width, more_sent, more_kept)
    small = jnp.concatenate(
        [first_sums[...], second_sums[...], third_sums[...], bias_sum[...],
         jnp.zeros((121, width), F32)], axis=0,
    )
    put_split(split, where[1], small.T, 2 * width, more_sent, more_kept)


def vision_back_kernel(where, q, kv, mixed, grad, probs, own, sent):
    width = q.shape[1]
    kv, probs = kv.wait(), probs.wait()

    @pl.when(where[0] == 0)
    def _():
        attend_back(q, 0, kv, 0, kv, width, mixed, grad, probs, sent, 0, own, 0, own, width)


def cross_back_kernel(where, q, kv, mixed, grad, probs, own, sent):
    width = kv.shape[1] // 2
    q, mixed, probs = q.wait(), mixed.wait(), probs.wait()

    @pl.when(where[0] == 0)
    def _():
        attend_back(q, 0, kv, 0, kv, width, mixed, grad, probs, own, 0, sent, 0, sent, width)


def cross_weight_kernel(
    split, place, own_query, own_key_value, query, key_value, x, dqkv, left, *outs
):
    sent, kept = outs if split else (None,) + outs
    width = own_query.shape[1]
    packed = query.shape[0]

    @pl.when(place[0] == 0)
    def _():
        dqkv[:, :width] = own_query[...]
        dqkv[:, width:] = own_key_value[...]

    @pl.when(place[0] != 0)
    def _():
        dqkv[:packed, :width] = query[...]
        dqkv[:packed, width:] = key_value[...]
        dqkv[packed:] = jnp.zeros((dqkv.shape[0] - packed, dqkv.shape[1]), BF16)

    left[...] = x.wait()[...].T
    for part in range(2):
        value = nn(left[...], dqkv[:, (1 + part) * width : (2 + part) * width])
        put_split(split, place[1], value, part * width, sent, kept)


def query_weight_kernel(split, place, left, dqkv, *outs):
    sent, kept = outs if split else (None,) + outs
    put_split(split, place[1], nn(left[...], dqkv[:, : left.shape[0]]), 0, sent, kept)


def feature_kernel(where, dqkv, first_grad, pick_t, wq, wkv, out, total):
    width = first_grad.shape[1]
    packed = pick_t.shape[1]
    total[...] = first_grad[...] + nt(dqkv[:, :width], wq.wait()[...])
    total[...] += nt(dqkv[:, width:], wkv.wait()[...])

    @pl.when(where[0] == 0)
    def _():
        out[...] = total[...]

    @pl.when(where[0] != 0)
    def _():
        value = total[:packed]
        high = value.astype(BF16)
        rest = (value - high.astype(F32)).astype(BF16)
        out[...] = nn(pick_t[...], high) + nn(pick_t[...], rest)


def to_partner(shard):
    return lax.ppermute(shard, "stream", [(0, 1), (1, 0)])


def to_language(shard):
    return lax.ppermute(shard, "stream", [(1, 0)])


def to_vision(shard):
    return lax.ppermute(shard, "stream", [(0, 1)])


def swap(shard, bit):
    count = lax.axis_size("docs")
    return lax.ppermute(shard, "docs", [(i, i ^ 1 << bit) for i in range(count)])


def after(value, *others):
    return lax.optimization_barrier((value,) + others)[0] if others else value


def combine_kernel(bit, where, kept, arrived, sent, rest):
    mine = (where[5] >> bit) & 1
    sent[...] = kept[:, 1 - mine] + arrived[:, 1 - mine]
    rest[...] = kept[:, mine] + arrived[:, mine]


def finish_kernel(parts, kept, arrived, *outs):
    for (start, stop), out in zip(parts, outs):
        out[...] = kept[:, start:stop].astype(F32) + arrived[:, start:stop].astype(F32)


def finish_more_kernel(kept, arrived, self_out, cross_out, gain, shift, gate):
    width = self_out.shape[1]
    for at, out in enumerate((self_out, cross_out)):
        cols = slice(at * width, (at + 1) * width)
        out[...] = kept[:, cols].astype(F32) + arrived[:, cols].astype(F32)
    small = (kept[:, 2 * width :].astype(F32) + arrived[:, 2 * width :].astype(F32)).T
    for row in range(3):
        gain[0, row : row + 1] = small[2 * row : 2 * row + 1]
        shift[0, row : row + 1] = small[2 * row + 1 : 2 * row + 2]
    gate[...] = small[6:7]


class Summation:
    def __init__(self, parts, first=0):
        index = lax.axis_index("docs")
        count = lax.axis_size("docs")
        self.names = list(range(count.bit_length() - 2, 0, -1))
        bits = list(range(1, count.bit_length() - 1))
        self.order = bits if first == 0 else bits[1:] + bits[:1]
        if len(parts) == 2:
            sent, kept = parts
        else:
            full = parts[0].reshape(count // 2, 2, -1, parts[0].shape[-1])
            core = index & 1
            sent = lax.dynamic_index_in_dim(full, 1 - core, 1, keepdims=False)
            kept = lax.dynamic_index_in_dim(full, core, 1, keepdims=False)
        self.kept = kept
        self.arrived = swap(sent, 0)

    def advance(self, *earlier):
        bit = self.order.pop(0)
        axis = self.names.index(bit)
        ahead, behind = 2**axis, 2 ** (len(self.names) - 1 - axis)
        self.names.pop(axis)
        tail = self.kept.shape[-2:]
        shape = (ahead, 2, behind) + tail
        half = ((ahead, behind) + tail, BF16, VM)
        self.sent, kept = run_kernel(
            functools.partial(combine_kernel, bit), "combine",
            [((), PLACE), (self.kept.reshape(shape), VM),
             (after(self.arrived, *earlier).reshape(shape), VM)],
            [half, half], us=1.0,
        )
        self.kept = kept
        self.arrived = swap(self.sent, bit)

    def last(self, *earlier):
        while self.order:
            self.advance(*earlier)
        shape = self.kept.shape[-2:]
        return [(self.kept.reshape(shape), VM), (after(self.arrived, *earlier).reshape(shape), VM)]

    def finish(self, parts, *earlier):
        operands = self.last(*earlier)
        shape = self.kept.shape[-2:]
        return run_kernel(
            functools.partial(finish_kernel, parts), "finish",
            operands,
            [((shape[0], stop - start), F32, VM) for start, stop in parts], us=1.0,
        )


def body(
    block_features, cotangent, text_counts, visual_counts, w_cross_q, w_cross_kv, w_cross_out,
    w_self_qkv, w_self_out, w_ffn_in, w_ffn_out, w_gate, ln_gain, ln_bias, gate_bias,
):
    feat = block_features[0]
    rows, width = feat.shape
    wq, wkv, wo = w_cross_q[0], w_cross_kv[0], w_cross_out[0]
    wqkv, ws = w_self_qkv[0], w_self_out[0]
    wi, wf, wg = w_ffn_in[0], w_ffn_out[0], w_gate[0]
    gains, shifts = ln_gain[0], ln_bias[0]
    hidden_width = wi.shape[1]
    count = lax.axis_size("docs")
    groups = count // 2
    split = (width // count) % 16 == 0
    packed = text_counts.shape[1] * SLOT
    heads = width // HD
    where = (text_counts, visual_counts)
    here = ()
    dma = pltpu.SemaphoreType.DMA
    low = ((rows, width), BF16, VM)
    wide = ((rows, width), F32, VM)
    sums = ((2, width), F32, VM)
    few = ((packed, width), BF16, VM)

    def weight_outs(total_rows, columns):
        if split:
            shape = (groups, total_rows // count, columns)
            return [(shape, BF16, VM), (shape, BF16, VM)]
        return [((total_rows, columns), BF16, VM)]

    parts = 2 if split else 1
    x, q, q_sent, pick, pick_t = run_kernel(
        query_kernel, "query",
        [(where, PLACE), (feat, LAZY), (wq, LAZY)],
        [low, low, few, ((packed, rows), BF16, VM), ((rows, packed), BF16, VM)],
        spare=48 << 20,
    )
    vision_q = to_language(q_sent)
    kv, kv_sent = run_kernel(
        key_value_kernel, "key_value",
        [(after(x, q_sent), VM), (wkv, VM)],
        [((rows, 2 * width), BF16, VM), ((packed, 2 * width), BF16, VM)],
    )
    vision_kv = to_language(kv_sent)
    vision_mixed, vision_probs = run_kernel(
        vision_attend_kernel, "vision_attend",
        [(where, PLACE), (vision_q, VM), (after(kv, kv_sent), VM)],
        [few, ((heads, rows, packed), BF16, VM)],
        [VM((rows, packed), F32)],
    )
    vision_mixed_here = to_vision(vision_mixed)
    own_mixed, cross_probs = run_kernel(
        own_attend_kernel, "own_attend",
        [(where, PLACE), (q, VM), (after(vision_kv, vision_mixed), VM)],
        [low, ((heads, packed, rows), BF16, VM)],
        [VM((packed, rows), F32)],
    )

    def state(*shape, kind=BF16):
        return (shape, kind, HBM)

    full = state(rows, width)
    lane = state(rows, 128, kind=F32)
    saved = [
        full, full, full, lane, state(rows, 3 * width), full, state(heads, rows, rows), full, full,
        lane, state(rows, hidden_width), state(rows, hidden_width), full, lane,
    ]
    (
        mixed, first_low, unit1, scale1, qkv, self_low, self_probs, second_low, unit2, scale2,
        hidden, slope, unit3, scale3, third, third_low, third_sent,
    ) = run_kernel(
        middle_kernel, "middle",
        [(where, PLACE), (x, VM), (own_mixed, VM), (after(vision_mixed_here, own_mixed), VM),
         (pick, VM), (gains, VM), (shifts, VM)] + [(w, LAZY) for w in (wo, wqkv, ws, wi, wf)],
        saved + [wide, low, few],
        [VM(shape, kind) for shape, kind, _ in saved]
        + [VM((rows, width), F32), VM((rows, rows), F32),
           dma((len(saved) - 2 + 2 * (hidden_width // FF_BLOCK),))],
        spare=VMEM_LIMIT,
    )
    other = to_partner(third_sent)
    own_logits, cot_rows = run_kernel(
        gate_own_kernel, "gate_own",
        [(here, PLACE), (after(third_low, third_sent), VM), (pick, VM), (cotangent[0], LAZY),
         (gate_bias, VM), (wg, VM)],
        [wide, low],
    )
    combined, other_low, logit_low, own_part, partner_sent, bias_sum = run_kernel(
        gate_kernel, "gate",
        [(where, PLACE), (third, VM), (after(other, own_logits), VM), (own_logits, VM),
         (cot_rows, VM), (pick, VM), (pick_t, VM), (wg, VM)],
        [wide, low, low, wide, few, ((1, width), F32, VM)],
    )
    returned = to_partner(partner_sent)
    gate_parts = run_kernel(
        functools.partial(gate_weight_kernel, split), "gate_weight",
        [(here, PLACE), (third_low, VM), (other_low, VM), (after(logit_low, partner_sent), VM)],
        weight_outs(2 * width, width),
    )
    gate_sum = Summation(gate_parts, 0)
    gate_sum.advance()
    third_back = run_kernel(
        functools.partial(third_back_kernel, split), "third_back",
        [(where, PLACE), (own_part, VM), (after(returned, gate_sum.sent), VM), (pick_t, VM),
         (unit3, LAZY), (scale3, LAZY), (gains, VM), (hidden, LAZY)],
        [wide, low, sums] + weight_outs(hidden_width, width),
        [VM((rows, width), F32)],
    )
    third_grad, third_grad_low, third_sums = third_back[:3]
    out_sum = Summation(third_back[3:], 0)
    ffn_back = run_kernel(
        functools.partial(ffn_back_kernel, split), "ffn_back",
        [(here, PLACE), (third_grad, VM), (after(third_grad_low, *third_back[3:]), VM), (wf, LAZY),
         (slope, LAZY), (second_low, LAZY), (wi, LAZY)],
        [wide] + weight_outs(width, hidden_width),
        [VM((width, rows), BF16)],
    )
    in_sum = Summation(ffn_back[1:], 0)
    out_sum.advance(ffn_back[0])
    second_grad, second_grad_low, mixed_grad, second_sums = run_kernel(
        second_back_kernel, "second_back",
        [(after(ffn_back[0], out_sum.sent, *ffn_back[1:]), VM), (unit2, LAZY), (scale2, LAZY),
         (gains, VM), (ws, LAZY)],
        [wide, low, low, sums],
    )
    in_sum.advance(second_sums)
    dqkv, first_grad, first_grad_low, cross_grad, cross_grad_sent, first_sums = run_kernel(
        self_back_kernel, "self_back",
        [(second_grad, VM), (after(mixed_grad, in_sum.sent), VM), (gains, VM),
         (qkv, LAZY), (self_low, LAZY), (self_probs, LAZY), (wqkv, LAZY), (unit1, LAZY),
         (scale1, LAZY), (wo, LAZY)],
        [((rows, 3 * width), BF16, VM), wide, low, low, few, sums],
    )
    vision_grad = to_language(cross_grad_sent)
    gate_sum.advance(first_sums)
    out_sum.advance(gate_sum.sent)
    self_parts = run_kernel(
        functools.partial(self_weight_kernel, split), "self_weight",
        [(here, PLACE), (after(dqkv, cross_grad_sent, out_sum.sent), VM), (second_grad_low, VM),
         (first_grad_low, VM), (first_sums, VM), (second_sums, VM), (third_sums, VM),
         (bias_sum, VM), (first_low, LAZY), (self_low, LAZY), (mixed, LAZY)],
        weight_outs(width, 3 * width) + weight_outs(width, 2 * width + 128),
    )
    self_sum = Summation(self_parts[:parts], 0)
    more_sum = Summation(self_parts[parts:], 0)
    gate_sum.advance(*self_parts)
    own_key_value, query_sent = run_kernel(
        vision_back_kernel, "vision_back",
        [(here, PLACE), (vision_q, VM), (kv, LAZY), (vision_mixed, VM),
         (after(vision_grad, gate_sum.sent, *self_parts), VM), (vision_probs, LAZY)],
        [((rows, 2 * width), BF16, VM), few],
    )
    query_here = to_vision(query_sent)
    self_sum.advance(query_sent)
    in_sum.advance(self_sum.sent)
    own_query, key_value_sent = run_kernel(
        cross_back_kernel, "cross_back",
        [(here, PLACE), (q, LAZY), (vision_kv, VM), (mixed, LAZY),
         (after(cross_grad, query_here, in_sum.sent), VM),
         (cross_probs, LAZY)],
        [low, ((packed, 2 * width), BF16, VM)],
    )
    key_value_here = to_vision(key_value_sent)
    more_sum.advance(key_value_sent)
    out_sum.advance(more_sum.sent)
    (gate_grad,) = gate_sum.finish([(0, width)], out_sum.sent)
    in_sum.advance(gate_grad)
    self_sum.advance(in_sum.sent)
    cross_out = run_kernel(
        functools.partial(cross_weight_kernel, split), "cross_weight",
        [(here, PLACE), (own_query, VM), (own_key_value, VM), (query_here, VM),
         (after(key_value_here, self_sum.sent), VM), (x, LAZY)],
        [((rows, 3 * width), BF16, VM), ((width, rows), BF16, VM)]
        + weight_outs(width, 2 * width),
    )
    dcross, left = cross_out[:2]
    cross_sum = Summation(cross_out[2:], 0)
    (feature_grad,) = run_kernel(
        feature_kernel, "feature",
        [(here, PLACE), (after(dcross, *cross_out[2:]), VM), (first_grad, VM), (pick_t, VM),
         (wq, LAZY), (wkv, LAZY)],
        [wide],
        [VM((rows, width), F32)],
    )
    cross_sum.advance(feature_grad)
    (ffn_out_grad,) = out_sum.finish([(0, width)], cross_sum.sent)
    last_parts = run_kernel(
        functools.partial(query_weight_kernel, split), "query_weight",
        [(here, PLACE), (left, VM), (after(dcross, ffn_out_grad), VM)],
        weight_outs(width, width),
    )
    last_sum = Summation(last_parts, 0)
    self_sum.advance(*last_parts)
    last_sum.advance(self_sum.sent)
    more_sum.advance(last_sum.sent)
    cross_sum.advance(more_sum.sent)
    (ffn_in_grad,) = in_sum.finish([(0, hidden_width)], cross_sum.sent)
    last_sum.advance(ffn_in_grad)
    (self_qkv_grad,) = self_sum.finish([(0, 3 * width)], last_sum.sent)
    more_sum.advance(self_qkv_grad)
    cross_sum.advance(more_sum.sent)
    last_sum.advance(cross_sum.sent)
    if split:
        piece = width // count
        self_out_grad, cross_out_grad, gain_grad, shift_grad, gate_bias_grad = run_kernel(
            finish_more_kernel, "finish_more", more_sum.last(last_sum.sent),
            [((piece, width), F32, VM)] * 2 + [((1, 3, piece), F32, VM)] * 2 + [((1, piece), F32, VM)],
            us=1.0,
        )
    else:
        self_out_grad, cross_out_grad, small = more_sum.finish(
            [(0, width), (width, 2 * width), (2 * width, 2 * width + 128)], last_sum.sent
        )
        small = small[:, :7].T
        gain_grad, shift_grad = small[None, 0:6:2], small[None, 1:6:2]
        gate_bias_grad = small[6:7]
    (cross_kv_grad,) = cross_sum.finish([(0, 2 * width)], self_out_grad)
    (cross_q_grad,) = last_sum.finish([(0, width)])
    return (
        combined[None],
        feature_grad[None],
        cross_q_grad[None],
        cross_kv_grad[None],
        cross_out_grad[None],
        self_qkv_grad[None],
        self_out_grad[None],
        ffn_in_grad[None],
        ffn_out_grad[None],
        gate_grad[None],
        gain_grad,
        shift_grad,
        gate_bias_grad,
    )


def solution(mesh):
    rows = P("stream", "docs", None)
    weight = P("stream", None, None)
    return jax.shard_map(
        body,
        mesh=mesh,
        in_specs=(rows, rows, P("docs", None), P("docs", None)) + (weight,) * 10
        + (P("stream", None),),
        out_specs=(rows,) * 10 + (P("stream", None, "docs"),) * 2 + (P("stream", "docs"),),
        check_vma=False,
    )
```
